32 devices in a mesh: chan: 4 (over y, x), facet: 8 (over z, core).
Axes of the slice: x: 2, y: 2, z: 4, core: 2. Of those that a mesh axis runs over, the one named last changes fastest.
Arguments:
- image_field: float32 [4, 2048, 2048], P('chan', 'facet'), may hold values from -6 to 6
- weights: bfloat16 [4, 2048, 2048], P('chan', None, 'facet'), may hold values from 0.049804688 to 1
- measured: bfloat16 [4, 2, 2048, 2048], P('chan', None, None, 'facet'), may hold values from -6 to 6
- dual_field: bfloat16 [4, 2, 2048, 2048], P(None, None, 'facet', 'chan'), may hold values from -3 to 3
Outputs:
- image_next: float32 [4, 2048, 2048], P(None, 'facet', 'chan')
- dual_next: bfloat16 [4, 2, 2048, 2048], P(None, None, 'facet', 'chan')
The draws below stay inside these ranges and needn't reach their ends.
All inputs are finite; a program needn't handle non-finite values.
Results may differ from the reference program's by a relative error of at most 0.001.
Values sent between devices are 32-bit elements; how exact they have to be, the bound alone decides.
A program may use at most 128 MiB of HBM per device.

```python
import math
import jax
import jax.numpy as jnp
from jax import lax

GRID = 2048
CHANNELS = 4


def block_levels(key, dims, split, low, top_value):
    loudness = 1.0
    for axis_at, shards_of in split:
        steps = jax.random.uniform(jax.random.fold_in(jax.random.fold_in(key, 6), axis_at), (shards_of,), jnp.float32, low / len(split), top_value / len(split))
        loudness = loudness * jnp.repeat(jnp.exp(steps), dims[axis_at] // shards_of).reshape((-1,) + (1,) * (len(dims) - 1 - axis_at))
    return loudness


def gaussian(own_key, shape, width, reach, split=(), dtype=jnp.bfloat16):
    drawn = width * jax.random.normal(own_key, shape, jnp.float32)
    if split:
        drawn = drawn * block_levels(own_key, shape, split, -0.22, 0.18)
    return jnp.clip(drawn, -reach, reach).astype(dtype)


def setup_inputs(seed: int = 0) -> dict:
    key_of = jax.random.split(jax.random.key(seed), 5)
    return {
        "image_field": gaussian(key_of[0], (CHANNELS, GRID, GRID), 1.0, 6.0, ((0, 4), (1, 8)), jnp.float32),
        "weights": jnp.clip(jnp.exp(math.log(1.0) - 2.9996462 * jax.random.uniform(key_of[1], (CHANNELS, GRID, GRID), jnp.float32) ** block_levels(key_of[1], (CHANNELS, GRID, GRID), ((0, 4), (2, 8)), -0.2, 0.2)), 0.049804688, 1.0).astype(jnp.bfloat16),
        "measured": gaussian(key_of[2], (CHANNELS, 2, GRID, GRID), 1.0, 6.0, ((0, 4), (3, 8))),
        "dual_field": gaussian(key_of[3], (CHANNELS, 2, GRID, GRID), 0.5, 3.0, ((2, 8), (3, 4))),
    }


step_primal = 0.5
step_dual = 0.5
clip_radius = 4.0

def reference(image_field, weights, measured, dual_field):

    def channel_gradient(inputs):
        channel_image, channel_weight, channel_data = inputs
        spectrum = jnp.fft.fft2(channel_image) / GRID
        residual = channel_weight.astype(jnp.float32) * spectrum - (channel_data[0].astype(jnp.float32) + 1j * channel_data[1].astype(jnp.float32))
        return jnp.real(jnp.fft.ifft2(residual)) * GRID
    gradient = lax.map(channel_gradient, (image_field, weights, measured))
    dual_rows = dual_field[:, 0].astype(jnp.float32)
    dual_cols = dual_field[:, 1].astype(jnp.float32)
    prev_rows = jnp.pad(dual_rows, ((0, 0), (1, 0), (0, 0)))[:, :-1, :]
    prev_cols = jnp.pad(dual_cols, ((0, 0), (0, 0), (1, 0)))[:, :, :-1]
    adjoint = prev_rows - dual_rows + prev_cols - dual_cols
    image_next = image_field - step_primal * (gradient + adjoint)
    extrapolated = 2.0 * image_next - image_field
    diff_rows = jnp.pad(extrapolated, ((0, 0), (0, 1), (0, 0)))[:, 1:, :] - extrapolated
    diff_cols = jnp.pad(extrapolated, ((0, 0), (0, 0), (0, 1)))[:, :, 1:] - extrapolated
    first_part = dual_rows + step_dual * diff_rows
    second_part = dual_cols + step_dual * diff_cols
    magnitude = jnp.sqrt(lax.optimization_barrier(jnp.sum(first_part * first_part + second_part * second_part, axis=0)))
    factor = 1.0 / jnp.maximum(1.0, magnitude / clip_radius)
    dual_next = jnp.stack([first_part * factor, second_part * factor], axis=1).astype(jnp.bfloat16)
    return (image_next, dual_next)
```

```python
from functools import partial
import math

import jax
import jax.numpy as jnp
import numpy as np
from jax import lax
from jax.experimental import pallas as pl
from jax.experimental.pallas import tpu as pltpu
from jax.sharding import PartitionSpec as P

step_primal = 0.5
step_dual = 0.5
clip_radius = 4.0
LANES = 128
BLOCK = 16


def turned(real, imag, num, den, sign):
    num = num % den
    if num == 0:
        return real, imag
    if 4 * num == den:
        return (-imag, real) if sign > 0 else (imag, -real)
    c = math.cos(2.0 * math.pi * num / den)
    s = sign * math.sin(2.0 * math.pi * num / den)
    if 8 * num == den:
        h = math.sqrt(0.5)
        if sign > 0:
            return (real - imag) * h, (real + imag) * h
        return (real + imag) * h, (imag - real) * h
    return real * c - imag * s, real * s + imag * c


def block_dft(values, sign):
    n = len(values)
    if n == 1:
        return values
    even = block_dft(values[0::2], sign)
    odd = block_dft(values[1::2], sign)
    low, high = [], []
    for k in range(n // 2):
        er, ei = even[k]
        tr, ti = turned(*odd[k], k, n, sign)
        low.append((er + tr, ei + ti))
        high.append((er - tr, ei - ti))
    return low + high


def halves(x):
    high = x.astype(jnp.bfloat16)
    return high, (x - high.astype(jnp.float32)).astype(jnp.bfloat16)


def exact_dot(first, second, dims):
    (fh, fl), (sh, sl) = first, second
    dot = partial(
        lax.dot_general, dimension_numbers=(dims, ((), ())), preferred_element_type=jnp.float32
    )
    return dot(fh, sh) + (dot(fh, sl) + dot(fl, sh))


def table_seeds(blocks, inner):
    n = blocks * inner
    a = np.arange(max(blocks, inner))[:, None]
    i = np.arange(inner)[None, :]

    def pairs(step, count):
        phase = 2.0 * np.pi / n * ((step * a[:count] * i) % n)
        pair = np.stack([np.cos(phase), -np.sin(phase)], axis=1).astype(np.float32)
        pair = pair.reshape(count, 2, inner // LANES, LANES)
        return pair.transpose(0, 2, 1, 3).reshape(count, 2 * inner)

    phase = 2.0 * np.pi / n * ((blocks * a[None, :inner] + a[:blocks, None]) * i[:, :LANES] % n)
    value = np.concatenate([np.cos(phase), -np.sin(phase)], axis=2).astype(np.float32)
    high = value.astype(jnp.bfloat16)
    low = (value - high.astype(np.float32)).astype(jnp.bfloat16)
    return pairs(blocks, inner), np.repeat(pairs(1, blocks)[:, None, :], 8, axis=1), np.stack([high, low])


def fill_tables(seed_ref, turn_ref, t_ref):
    _, F, A, width = t_ref.shape

    @pl.loop(0, F)
    def _(b):
        for c in range(1, width // (2 * LANES)):
            re_at = slice(2 * c * LANES, (2 * c + 1) * LANES)
            im_at = slice((2 * c + 1) * LANES, (2 * c + 2) * LANES)
            turn_re, turn_im = turn_ref[b, 0:1, re_at], turn_ref[b, 0:1, im_at]

            @pl.loop(0, A // 32)
            def _(t):
                rows = pl.ds(pl.multiple_of(t * 32, 32), 32)
                re, im = seed_ref[rows, re_at], seed_ref[rows, im_at]
                pair = (re * turn_re - im * turn_im, re * turn_im + im * turn_re)
                for value, at in zip(pair, (re_at, im_at)):
                    high, low = halves(value)
                    t_ref[0, b, rows, at] = high
                    t_ref[1, b, rows, at] = low


def back_pieces(rows):
    pieces, start = [], 0
    for part in (4, 4, 4, 8, 8):
        pieces.append((start, rows // part))
        start += rows // part
    return pieces


def square_tables(t_ref, k, chunks):
    found = []
    for at in (0, LANES):
        pieces = [
            [t_ref[s, k, :, 2 * LANES * c + at:2 * LANES * c + at + LANES] for c in range(chunks)]
            for s in (0, 1)
        ]
        found.append(tuple(jnp.concatenate(p, axis=1) if chunks > 1 else p[0] for p in pieces))
    return found


def halo_copy(source, target, send_sem, recv_sem, device):
    return pltpu.make_async_remote_copy(
        src_ref=source, dst_ref=target, send_sem=send_sem, recv_sem=recv_sem,
        device_id=device, device_id_type=pl.DeviceIdType.MESH,
    )


def kernel(
    F, CH, x_hbm, seed_ref, turn_ref, table_hbm, w_hbm, m_hbm, d_hbm,
    image_hbm, next_hbm,
    t_ref, x_ref, image_ref, grad_ref, dual, up, up_ref, low, low_ref,
    left, left_ref, right, right_ref, edge, edge_ref, column, parts,
    xt, z, send, recv, wb, mb, wf, mf, u, sendy, recvy, gt, g,
    in_sem, fs, fr, bs, br, cs, cr, xs, xr, ls, hs, hr, rs, rr, out_sem,
):
    R, N = x_ref.shape
    A = N // F
    C = A // LANES
    T = N // CH
    RC = R // LANES
    W = 2 * LANES
    scale = 1.0 / N
    me = lax.axis_index("facet")
    mine = lax.axis_index("chan")
    order = sorted(range(1, F), key=lambda o: abs(o - F // 2))

    load_x = [
        pltpu.make_async_copy(
            x_hbm.at[h * LANES:(h + 1) * LANES], x_ref.at[h * LANES:(h + 1) * LANES],
            in_sem.at[6 + h],
        )
        for h in range(RC)
    ]
    load_t = pltpu.make_async_copy(table_hbm, t_ref.at[:, :, :, 0:W], in_sem.at[6 + RC])
    load_x[0].start()
    load_t.start()
    for copy in load_x[1:]:
        copy.start()
    load_w = pltpu.make_async_copy(w_hbm.at[0], wb, in_sem.at[0])
    load_m = pltpu.make_async_copy(m_hbm.at[0], mb, in_sem.at[1])
    load_w.start()
    load_m.start()
    load_d = pltpu.make_async_copy(d_hbm, dual, in_sem.at[2])
    load_d.start()
    above, below = lax.rem(me + F - 1, F), lax.rem(me + 1, F)
    before, after = lax.rem(mine + CH - 1, CH), lax.rem(mine + 1, CH)

    barrier = pltpu.get_barrier_semaphore()
    for o in range(1, F):
        pl.semaphore_signal(
            barrier, inc=1, device_id={"facet": lax.rem(me + o, F)},
            device_id_type=pl.DeviceIdType.MESH,
        )
    for o in range(1, CH):
        pl.semaphore_signal(
            barrier, inc=1, device_id={"chan": lax.rem(mine + o, CH)},
            device_id_type=pl.DeviceIdType.MESH,
        )

    copies = []
    for c in range(C):
        wide = slice(c * W, (c + 1) * W)
        group = []
        for h in range(RC):
            if c == 0:
                load_x[h].wait()
                for j in range(N // LANES):
                    xt[h, j * LANES:(j + 1) * LANES, :] = x_ref[
                        h * LANES:(h + 1) * LANES, j * LANES:(j + 1) * LANES
                    ].T

            if c == 0 and h == 0:
                load_t.wait()

            @pl.loop(0, F)
            def _(b):
                part = halves(xt[h, pl.ds(b, A, stride=F), :].T)
                table = (t_ref[0, b, :, wide], t_ref[1, b, :, wide])
                z[b, 0:LANES, 0:W] = exact_dot(part, table, ((1,), (0,)))

            @pl.loop(0, LANES // 8)
            def _(t):
                rows = pl.ds(pl.multiple_of(t * 8, 8), 8)
                target = pl.ds(pl.multiple_of(h * LANES + t * 8, 8), 8)
                values = [(z[b, rows, 0:LANES], z[b, rows, LANES:W]) for b in range(F)]
                for j, (re, im) in enumerate(block_dft(values, -1.0)):
                    send[c, j, target, 0:LANES] = re
                    send[c, j, target, LANES:W] = im

            if c == 0 and h == 0:
                pl.semaphore_wait(barrier, F - 1 + CH - 1)
            span = pl.ds(h * LANES, LANES)
            for o in order:
                d = lax.rem(me + o, F)
                copy = pltpu.make_async_remote_copy(
                    src_ref=send.at[c, d, span], dst_ref=recv.at[c, me, span],
                    send_sem=fs.at[c, h, o], recv_sem=fr.at[c, h, o],
                    device_id={"facet": d}, device_id_type=pl.DeviceIdType.MESH,
                )
                copy.start()
                group.append(copy)
            copy = pltpu.make_async_copy(
                send.at[c, me, span], recv.at[c, me, span], fr.at[c, h, 0]
            )
            copy.start()
            group.append(copy)
        copies.append(group)
        if c == 0:
            fill_tables(seed_ref, turn_ref, t_ref)
            load_d.wait()
            for k in range(CH):
                up[k:k + 1, :] = dual[k, 0, R - 16:R, :].astype(jnp.float32)[15:16, :]
                left[k] = dual[k, 1, :, T - LANES:T].astype(jnp.float32)
            halos = [
                halo_copy(up, up_ref, hs.at[0], hr.at[0], {"facet": below}),
                halo_copy(left, left_ref, hs.at[1], hr.at[1], {"chan": after}),
            ]
            for copy in halos:
                copy.start()

            image_copies = []
            for o in range(1, CH):
                d = lax.rem(mine + o, CH)
                copy = pltpu.make_async_remote_copy(
                    src_ref=x_ref.at[:, pl.ds(pl.multiple_of(d * T, LANES), T)],
                    dst_ref=image_ref.at[mine, 0:R],
                    send_sem=xs.at[o], recv_sem=xr.at[o],
                    device_id={"chan": d}, device_id_type=pl.DeviceIdType.MESH,
                )
                copy.start()
                image_copies.append(copy)
            own = pltpu.make_async_copy(
                x_ref.at[:, pl.ds(pl.multiple_of(mine * T, LANES), T)], image_ref.at[mine, 0:R], ls.at[0]
            )
            own.start()
            image_copies.append(own)

    load_w.wait()
    load_m.wait()

    @pl.loop(0, N // 16)
    def _(t):
        rows = pl.ds(pl.multiple_of(t * 16, 16), 16)
        for c in range(C):
            lo = c * LANES
            wf[c, rows, :] = wb[rows, lo:lo + LANES].astype(jnp.float32) * scale
            mf[c, 0, rows, :] = mb[0, rows, lo:lo + LANES].astype(jnp.float32)
            mf[c, 1, rows, :] = mb[1, rows, lo:lo + LANES].astype(jnp.float32)

    pieces = back_pieces(R)
    back = [[] for _ in pieces]
    for c in range(C):
        wide = slice(c * W, (c + 1) * W)
        for copy in copies[c]:
            copy.wait()

        @pl.loop(0, R // 8)
        def _(t):
            rows = pl.ds(pl.multiple_of(t * 8, 8), 8)
            values = [(recv[c, q, rows, 0:LANES], recv[c, q, rows, LANES:W]) for q in range(F)]
            for k, (re, im) in enumerate(block_dft(values, -1.0)):
                u[k, rows, 0:LANES] = re
                u[k, rows, LANES:W] = im

        @pl.loop(0, F)
        def _(k):
            cos, sin = square_tables(t_ref, k, C)
            part = halves(u[k])
            p = exact_dot(cos, part, ((1,), (0,)))
            q = exact_dot(sin, part, ((1,), (0,)))
            spec_re = p[:, 0:LANES] - q[:, LANES:]
            spec_im = p[:, LANES:] + q[:, 0:LANES]
            lines = pl.ds(k, A, stride=F)
            weight = wf[c, lines, :]
            res_re = weight * spec_re - mf[c, 0, lines, :]
            res_im = weight * spec_im - mf[c, 1, lines, :]
            part = halves(jnp.concatenate([res_re, res_im], axis=1))
            p = exact_dot(cos, part, ((0,), (0,)))
            q = exact_dot(sin, part, ((0,), (0,)))
            u[k, :, 0:LANES] = p[:, 0:LANES] + q[:, LANES:]
            u[k, :, LANES:W] = p[:, LANES:] - q[:, 0:LANES]

        for i, (start, size) in enumerate(pieces if c == C - 1 else [(0, R)]):

            @pl.loop(0, size // 8)
            def _(t):
                rows = pl.ds(pl.multiple_of(start + t * 8, 8), 8)
                values = [(u[k, rows, 0:LANES], u[k, rows, LANES:W]) for k in range(F)]
                for q, (re, im) in enumerate(block_dft(values, 1.0)):
                    sendy[q, rows, c * W:c * W + LANES] = re
                    sendy[q, rows, c * W + LANES:(c + 1) * W] = im

            span = pl.ds(start, size)
            for o in order:
                d = lax.rem(me + o, F)
                copy = pltpu.make_async_remote_copy(
                    src_ref=sendy.at[d, span, wide], dst_ref=recvy.at[me, span, wide],
                    send_sem=bs.at[c, i, o], recv_sem=br.at[c, i, o],
                    device_id={"facet": d}, device_id_type=pl.DeviceIdType.MESH,
                )
                copy.start()
                back[i].append(copy)
            copy = pltpu.make_async_copy(
                sendy.at[me, span, wide], recvy.at[me, span, wide], br.at[c, i, 0]
            )
            copy.start()
            back[i].append(copy)

        if c == 0:
            for copy in image_copies + halos:
                copy.wait()
            for k in range(CH):
                first_up = jnp.where(me > 0, up_ref[k:k + 1, 0:LANES], 0.0)
                first_left = jnp.where(mine > 0, left_ref[k], 0.0)[:, LANES - 1:LANES]
                p = dual[k, 0, :, 0:LANES].astype(jnp.float32)
                q = dual[k, 1, :, 0:LANES].astype(jnp.float32)
                row = lax.broadcasted_iota(jnp.int32, (R, LANES), 0)
                p_prev = jnp.where(row == 0, first_up, pltpu.roll(p, 1, 0))
                right[k] = image_ref[k, 0:R, 0:LANES] - (p_prev - p + first_left - q)
            edges = [halo_copy(right, right_ref, hs.at[3], hr.at[3], {"chan": before})]
            for copy in edges:
                copy.start()

    row = lax.broadcasted_iota(jnp.int32, (BLOCK, T), 0)
    lane = lax.broadcasted_iota(jnp.int32, (BLOCK, T), 1)

    def primal(first, end):
        @pl.loop(first, end)
        def _(at):
            rows = pl.ds(pl.multiple_of(at * BLOCK, BLOCK), BLOCK)
            ahead = pl.ds(pl.multiple_of(jnp.maximum(at - 1, 0) * BLOCK, BLOCK), BLOCK)
            for k in range(CH):
                p = dual[k, 0, rows, :].astype(jnp.float32)
                q = dual[k, 1, rows, :].astype(jnp.float32)
                top = dual[k, 0, ahead, :].astype(jnp.float32)[BLOCK - 1:BLOCK, :]
                top = jnp.where(at > 0, top, jnp.where(me > 0, up_ref[k:k + 1, :], 0.0))
                p_prev = jnp.where(row == 0, top, pltpu.roll(p, 1, 0))
                start = jnp.where(mine > 0, left_ref[k, rows, :], 0.0)[:, LANES - 1:LANES]
                q_prev = jnp.where(lane == 0, start, pltpu.roll(q, 1, 1))
                adjoint = p_prev - p + q_prev - q
                x = image_ref[k, rows, :]
                value = x - step_primal * (grad_ref[k, rows, :] + adjoint)
                grad_ref[k, rows, :] = value
                image_ref[k, rows, :] = 2.0 * value - x

    def shrink(first, end):
        @pl.loop(first, end)
        def _(at):
            rows = pl.ds(pl.multiple_of(at * BLOCK, BLOCK), BLOCK)
            later = pl.ds(pl.multiple_of(at * BLOCK + BLOCK, BLOCK), 8)
            total = jnp.zeros((BLOCK, T), jnp.float32)
            for k in range(CH):
                e = image_ref[k, rows, :]
                following = image_ref[k, later, :][0:1, :]
                down = jnp.where(row == BLOCK - 1, following, pltpu.roll(e, BLOCK - 1, 0)) - e
                side = right_ref[k, rows, :][:, 0:1] - column[rows, :][:, k:k + 1]
                side = jnp.where(mine < CH - 1, side, 0.0)
                over = jnp.where(lane == T - 1, side, pltpu.roll(e, T - 1, 1)) - e
                first_part = dual[k, 0, rows, :].astype(jnp.float32) + step_dual * down
                second_part = dual[k, 1, rows, :].astype(jnp.float32) + step_dual * over
                parts[k, 0] = first_part
                parts[k, 1] = second_part
                total = total + (first_part * first_part + second_part * second_part)
            factor = 1.0 / jnp.maximum(1.0, jnp.sqrt(total) / clip_radius)
            for k in range(CH):
                dual[k, 0, rows, :] = (parts[k, 0] * factor).astype(jnp.bfloat16)
                dual[k, 1, rows, :] = (parts[k, 1] * factor).astype(jnp.bfloat16)

    last = [[] for _ in pieces]
    outs = []

    def finish(h):
        start, size = pieces[h]
        for copy in last[h]:
            copy.wait()
        if h == 0:
            for copy in edges:
                copy.wait()
        tile = jnp.concatenate([edge_ref[k, h, 0:1, :] for k in range(CH)], axis=0)
        tile = jnp.concatenate([tile] * (LANES // CH), axis=0)
        column[start:start + size, :] = tile.T[0:size, :]
        primal(start // BLOCK, (start + size) // BLOCK)
        if h == 0:
            for k in range(CH):
                low[k:k + 1, :] = image_ref[k, 0:8, :][0:1, :]
            copy = halo_copy(low, low_ref, hs.at[2], hr.at[2], {"facet": above})
            copy.start()
            edges.append(copy)
        final = h == len(pieces) - 1
        if final:
            edges[-1].wait()
            for k in range(CH):
                image_ref[k, R:R + 1, :] = jnp.where(me < F - 1, low_ref[k:k + 1, :], 0.0)
        first = max(start // BLOCK - 1, 0)
        end = (start + size) // BLOCK - (0 if final else 1)
        shrink(first, end)
        done = slice(start, start + size)
        outs.append(pltpu.make_async_copy(
            grad_ref.at[:, done, :], image_hbm.at[:, done, :], out_sem.at[0, h]
        ))
        done = slice(first * BLOCK, end * BLOCK)
        outs.append(pltpu.make_async_copy(
            dual.at[:, :, done, :], next_hbm.at[:, :, done, :], out_sem.at[1, h]
        ))
        for copy in outs[-2:]:
            copy.start()

    for h, (start, size) in enumerate(pieces):
        for copy in back[h]:
            copy.wait()

        @pl.loop(0, size // 8)
        def _(t):
            rows = pl.ds(pl.multiple_of(start + t * 8, 8), 8)
            target = pl.ds(pl.multiple_of(t * 8, 8), 8)
            for c in range(C):
                re_at, im_at = pl.ds(c * W, LANES), pl.ds(c * W + LANES, LANES)
                values = [(recvy[j, rows, re_at], recvy[j, rows, im_at]) for j in range(F)]
                for b, (re, im) in enumerate(block_dft(values, 1.0)):
                    z[b, target, re_at] = re
                    z[b, target, im_at] = im

        span = pl.ds(start, size)

        @pl.loop(0, F)
        def _(b):
            line = exact_dot((t_ref[0, b], t_ref[1, b]), halves(z[b]), ((1,), (1,)))
            gt[pl.ds(b, A, stride=F), :] = line * scale

        for e in range(CH):
            edge[h, e] = gt[e * T:e * T + 8, :]
        for j in range(N // LANES):
            g[span, j * LANES:(j + 1) * LANES] = gt[j * LANES:(j + 1) * LANES, :].T[0:size, :]
        for o in range(1, CH):
            d = lax.rem(mine + o, CH)
            last[h].append(pltpu.make_async_remote_copy(
                src_ref=g.at[span, pl.ds(pl.multiple_of(d * T, LANES), T)],
                dst_ref=grad_ref.at[mine, span],
                send_sem=cs.at[h, o], recv_sem=cr.at[h, o],
                device_id={"chan": d}, device_id_type=pl.DeviceIdType.MESH,
            ))
            last[h].append(halo_copy(
                edge.at[h, lax.rem(mine + o + 1, CH)], edge_ref.at[mine, h],
                rs.at[h, o], rr.at[h, o], {"chan": d},
            ))
        last[h].append(pltpu.make_async_copy(
            g.at[span, pl.ds(pl.multiple_of(mine * T, LANES), T)],
            grad_ref.at[mine, span], ls.at[1 + h],
        ))
        last[h].append(pltpu.make_async_copy(
            edge.at[h, after], edge_ref.at[mine, h], rr.at[h, 0]
        ))
        for copy in last[h]:
            copy.start()
        if h > 0:
            finish(h - 1)
    finish(len(pieces) - 1)
    for copy in outs:
        copy.wait()


def shards(image, weights, measured, dual):
    F, CH = lax.axis_size("facet"), lax.axis_size("chan")
    R, N = image.shape[1:]
    A = N // F
    C = A // LANES
    RC = R // LANES
    seed, turn, table = (jnp.asarray(t) for t in table_seeds(F, A))
    PC = len(back_pieces(R))
    T = N // CH
    HR = -(-CH // 8) * 8
    f32 = jnp.float32
    dma = pltpu.SemaphoreType.DMA
    vmem = pl.BlockSpec(memory_space=pltpu.VMEM)
    hbm = pl.BlockSpec(memory_space=pl.ANY)
    return pl.pallas_call(
        partial(kernel, F, CH),
        out_shape=(
            jax.ShapeDtypeStruct((CH, R, T), f32),
            jax.ShapeDtypeStruct((CH, 2, R, T), jnp.bfloat16),
        ),
        in_specs=[hbm, vmem, vmem, hbm, hbm, hbm, hbm],
        out_specs=(hbm, hbm),
        scratch_shapes=[
            pltpu.VMEM((2, F, A, 2 * A), jnp.bfloat16),
            pltpu.VMEM((R, N), f32),
            pltpu.VMEM((CH, R + 8, T), f32),
            pltpu.VMEM((CH, R, T), f32),
            pltpu.VMEM((CH, 2, R, T), jnp.bfloat16),
            pltpu.VMEM((HR, T), f32),
            pltpu.VMEM((HR, T), f32),
            pltpu.VMEM((HR, T), f32),
            pltpu.VMEM((HR, T), f32),
            pltpu.VMEM((CH, R, LANES), f32),
            pltpu.VMEM((CH, R, LANES), f32),
            pltpu.VMEM((CH, R, LANES), f32),
            pltpu.VMEM((CH, R, LANES), f32),
            pltpu.VMEM((PC, CH, 8, LANES), f32),
            pltpu.VMEM((CH, PC, 8, LANES), f32),
            pltpu.VMEM((R, LANES), f32),
            pltpu.VMEM((CH, 2, BLOCK, T), f32),
            pltpu.VMEM((RC, N, LANES), f32),
            pltpu.VMEM((F, LANES, 2 * A), f32),
            pltpu.VMEM((C, F, R, 2 * LANES), f32),
            pltpu.VMEM((C, F, R, 2 * LANES), f32),
            pltpu.VMEM((N, A), jnp.bfloat16),
            pltpu.VMEM((2, N, A), jnp.bfloat16),
            pltpu.VMEM((C, N, LANES), f32),
            pltpu.VMEM((C, 2, N, LANES), f32),
            pltpu.VMEM((F, A, 2 * LANES), f32),
            pltpu.VMEM((F, R, 2 * A), f32),
            pltpu.VMEM((F, R, 2 * A), f32),
            pltpu.VMEM((N, LANES), f32),
            pltpu.VMEM((R, N), f32),
            dma((7 + RC,)),
            dma((C, RC, F)), dma((C, RC, F)),
            dma((C, PC, F)), dma((C, PC, F)),
            dma((PC, CH)), dma((PC, CH)),
            dma((CH,)), dma((CH,)),
            dma((1 + PC,)),
            dma((4,)), dma((4,)),
            dma((PC, CH)), dma((PC, CH)),
            dma((2, PC)),
        ],
        compiler_params=pltpu.CompilerParams(
            collective_id=0, has_side_effects=True, vmem_limit_bytes=60 * 1024 * 1024
        ),
    )(image[0], seed, turn, table, weights, measured, dual)


def solution(mesh):
    placed = (
        P("chan", "facet", None),
        P("chan", None, "facet"),
        P("chan", None, None, "facet"),
        P(None, None, "facet", "chan"),
    )
    return jax.shard_map(
        shards,
        mesh=mesh,
        in_specs=placed,
        out_specs=(P(None, "facet", "chan"), P(None, None, "facet", "chan")),
        check_vma=False,
    )
```

```python
from functools import partial
import math

import jax
import jax.numpy as jnp
import numpy as np
from jax import lax
from jax.experimental import pallas as pl
from jax.experimental.pallas import tpu as pltpu
from jax.sharding import PartitionSpec as P

step_primal = 0.5
step_dual = 0.5
clip_radius = 4.0
LANES = 128
BLOCK = 16


def turned(real, imag, num, den, sign):
    num = num % den
    if num == 0:
        return real, imag
    if 4 * num == den:
        return (-imag, real) if sign > 0 else (imag, -real)
    c = math.cos(2.0 * math.pi * num / den)
    s = sign * math.sin(2.0 * math.pi * num / den)
    if 8 * num == den:
        h = math.sqrt(0.5)
        if sign > 0:
            return (real - imag) * h, (real + imag) * h
        return (real + imag) * h, (imag - real) * h
    return real * c - imag * s, real * s + imag * c


def block_dft(values, sign):
    n = len(values)
    if n == 1:
        return values
    even = block_dft(values[0::2], sign)
    odd = block_dft(values[1::2], sign)
    low, high = [], []
    for k in range(n // 2):
        er, ei = even[k]
        tr, ti = turned(*odd[k], k, n, sign)
        low.append((er + tr, ei + ti))
        high.append((er - tr, ei - ti))
    return low + high


def halves(x):
    high = x.astype(jnp.bfloat16)
    return high, (x - high.astype(jnp.float32)).astype(jnp.bfloat16)


def exact_dot(first, second, dims):
    (fh, fl), (sh, sl) = first, second
    dot = partial(
        lax.dot_general, dimension_numbers=(dims, ((), ())), preferred_element_type=jnp.float32
    )
    return dot(fh, sh) + (dot(fh, sl) + dot(fl, sh))


def table_seeds(blocks, inner):
    n = blocks * inner
    a = np.arange(max(blocks, inner))[:, None]
    i = np.arange(inner)[None, :]

    def pairs(step, count):
        phase = 2.0 * np.pi / n * ((step * a[:count] * i) % n)
        pair = np.stack([np.cos(phase), -np.sin(phase)], axis=1).astype(np.float32)
        pair = pair.reshape(count, 2, inner // LANES, LANES)
        return pair.transpose(0, 2, 1, 3).reshape(count, 2 * inner)

    phase = 2.0 * np.pi / n * ((blocks * a[None, :inner] + a[:blocks, None]) * i[:, :LANES] % n)
    value = np.concatenate([np.cos(phase), -np.sin(phase)], axis=2).astype(np.float32)
    high = value.astype(jnp.bfloat16)
    low = (value - high.astype(np.float32)).astype(jnp.bfloat16)
    return pairs(blocks, inner), np.repeat(pairs(1, blocks)[:, None, :], 8, axis=1), np.stack([high, low])


def fill_tables(seed_ref, turn_ref, t_ref):
    _, F, A, width = t_ref.shape

    @pl.loop(0, F)
    def _(b):
        for c in range(1, width // (2 * LANES)):
            re_at = slice(2 * c * LANES, (2 * c + 1) * LANES)
            im_at = slice((2 * c + 1) * LANES, (2 * c + 2) * LANES)
            turn_re, turn_im = turn_ref[b, 0:1, re_at], turn_ref[b, 0:1, im_at]

            @pl.loop(0, A // 32)
            def _(t):
                rows = pl.ds(pl.multiple_of(t * 32, 32), 32)
                re, im = seed_ref[rows, re_at], seed_ref[rows, im_at]
                pair = (re * turn_re - im * turn_im, re * turn_im + im * turn_re)
                for value, at in zip(pair, (re_at, im_at)):
                    high, low = halves(value)
                    t_ref[0, b, rows, at] = high
                    t_ref[1, b, rows, at] = low


def back_pieces(rows):
    pieces, start = [], 0
    for part in (4, 4, 4, 8, 8):
        pieces.append((start, rows // part))
        start += rows // part
    return pieces


def square_tables(t_ref, k, chunks):
    found = []
    for at in (0, LANES):
        pieces = [
            [t_ref[s, k, :, 2 * LANES * c + at:2 * LANES * c + at + LANES] for c in range(chunks)]
            for s in (0, 1)
        ]
        found.append(tuple(jnp.concatenate(p, axis=1) if chunks > 1 else p[0] for p in pieces))
    return found


def halo_copy(source, target, send_sem, recv_sem, device):
    return pltpu.make_async_remote_copy(
        src_ref=source, dst_ref=target, send_sem=send_sem, recv_sem=recv_sem,
        device_id=device, device_id_type=pl.DeviceIdType.MESH,
    )


def kernel(
    F, CH, x_hbm, seed_ref, turn_ref, table_hbm, w_hbm, m_hbm, d_hbm,
    grad_ref, dual,
    t_ref, x_ref, image_ref, up, up_ref, low, low_ref,
    left, left_ref, right, right_ref, edge, edge_ref, column, parts,
    xt, z, send, recv, wb, mb, wf, mf, u, sendy, recvy, gt, g,
    in_sem, fs, fr, bs, br, cs, cr, xs, xr, ls, hs, hr, rs, rr,
):
    R, N = x_ref.shape
    A = N // F
    C = A // LANES
    T = N // CH
    RC = R // LANES
    W = 2 * LANES
    scale = 1.0 / N
    me = lax.axis_index("facet")
    mine = lax.axis_index("chan")
    order = sorted(range(1, F), key=lambda o: abs(o - F // 2))

    load_x = [
        pltpu.make_async_copy(
            x_hbm.at[h * LANES:(h + 1) * LANES], x_ref.at[h * LANES:(h + 1) * LANES],
            in_sem.at[6 + h],
        )
        for h in range(RC)
    ]
    load_t = pltpu.make_async_copy(table_hbm, t_ref.at[:, :, :, 0:W], in_sem.at[6 + RC])
    load_x[0].start()
    load_t.start()
    for copy in load_x[1:]:
        copy.start()
    load_w = pltpu.make_async_copy(w_hbm.at[0], wb, in_sem.at[0])
    load_m = pltpu.make_async_copy(m_hbm.at[0], mb, in_sem.at[1])
    load_w.start()
    load_m.start()
    load_d = pltpu.make_async_copy(d_hbm, dual, in_sem.at[2])
    load_d.start()
    above, below = lax.rem(me + F - 1, F), lax.rem(me + 1, F)
    before, after = lax.rem(mine + CH - 1, CH), lax.rem(mine + 1, CH)

    barrier = pltpu.get_barrier_semaphore()
    for o in range(1, F):
        pl.semaphore_signal(
            barrier, inc=1, device_id={"facet": lax.rem(me + o, F)},
            device_id_type=pl.DeviceIdType.MESH,
        )
    for o in range(1, CH):
        pl.semaphore_signal(
            barrier, inc=1, device_id={"chan": lax.rem(mine + o, CH)},
            device_id_type=pl.DeviceIdType.MESH,
        )

    copies = []
    for c in range(C):
        wide = slice(c * W, (c + 1) * W)
        group = []
        for h in range(RC):
            if c == 0:
                load_x[h].wait()
                for j in range(N // LANES):
                    xt[h, j * LANES:(j + 1) * LANES, :] = x_ref[
                        h * LANES:(h + 1) * LANES, j * LANES:(j + 1) * LANES
                    ].T

            if c == 0 and h == 0:
                load_t.wait()

            @pl.loop(0, F)
            def _(b):
                part = halves(xt[h, pl.ds(b, A, stride=F), :].T)
                table = (t_ref[0, b, :, wide], t_ref[1, b, :, wide])
                z[b, 0:LANES, 0:W] = exact_dot(part, table, ((1,), (0,)))

            @pl.loop(0, LANES // 8)
            def _(t):
                rows = pl.ds(pl.multiple_of(t * 8, 8), 8)
                target = pl.ds(pl.multiple_of(h * LANES + t * 8, 8), 8)
                values = [(z[b, rows, 0:LANES], z[b, rows, LANES:W]) for b in range(F)]
                for j, (re, im) in enumerate(block_dft(values, -1.0)):
                    send[c, j, target, 0:LANES] = re
                    send[c, j, target, LANES:W] = im

            if c == 0 and h == 0:
                pl.semaphore_wait(barrier, F - 1 + CH - 1)
            span = pl.ds(h * LANES, LANES)
            for o in order:
                d = lax.rem(me + o, F)
                copy = pltpu.make_async_remote_copy(
                    src_ref=send.at[c, d, span], dst_ref=recv.at[c, me, span],
                    send_sem=fs.at[c, h, o], recv_sem=fr.at[c, h, o],
                    device_id={"facet": d}, device_id_type=pl.DeviceIdType.MESH,
                )
                copy.start()
                group.append(copy)
            copy = pltpu.make_async_copy(
                send.at[c, me, span], recv.at[c, me, span], fr.at[c, h, 0]
            )
            copy.start()
            group.append(copy)
        copies.append(group)
        if c == 0:
            fill_tables(seed_ref, turn_ref, t_ref)
            load_d.wait()
            for k in range(CH):
                up[k:k + 1, :] = dual[k, 0, R - 16:R, :].astype(jnp.float32)[15:16, :]
                left[k] = dual[k, 1, :, T - LANES:T].astype(jnp.float32)
            halos = [
                halo_copy(up, up_ref, hs.at[0], hr.at[0], {"facet": below}),
                halo_copy(left, left_ref, hs.at[1], hr.at[1], {"chan": after}),
            ]
            for copy in halos:
                copy.start()

            image_copies = []
            for o in range(1, CH):
                d = lax.rem(mine + o, CH)
                copy = pltpu.make_async_remote_copy(
                    src_ref=x_ref.at[:, pl.ds(pl.multiple_of(d * T, LANES), T)],
                    dst_ref=image_ref.at[mine, 0:R],
                    send_sem=xs.at[o], recv_sem=xr.at[o],
                    device_id={"chan": d}, device_id_type=pl.DeviceIdType.MESH,
                )
                copy.start()
                image_copies.append(copy)
            own = pltpu.make_async_copy(
                x_ref.at[:, pl.ds(pl.multiple_of(mine * T, LANES), T)], image_ref.at[mine, 0:R], ls.at[0]
            )
            own.start()
            image_copies.append(own)

    load_w.wait()
    load_m.wait()

    @pl.loop(0, N // 16)
    def _(t):
        rows = pl.ds(pl.multiple_of(t * 16, 16), 16)
        for c in range(C):
            lo = c * LANES
            wf[c, rows, :] = wb[rows, lo:lo + LANES].astype(jnp.float32) * scale
            mf[c, 0, rows, :] = mb[0, rows, lo:lo + LANES].astype(jnp.float32)
            mf[c, 1, rows, :] = mb[1, rows, lo:lo + LANES].astype(jnp.float32)

    pieces = back_pieces(R)
    back = [[] for _ in pieces]
    for c in range(C):
        wide = slice(c * W, (c + 1) * W)
        for copy in copies[c]:
            copy.wait()

        @pl.loop(0, R // 8)
        def _(t):
            rows = pl.ds(pl.multiple_of(t * 8, 8), 8)
            values = [(recv[c, q, rows, 0:LANES], recv[c, q, rows, LANES:W]) for q in range(F)]
            for k, (re, im) in enumerate(block_dft(values, -1.0)):
                u[k, rows, 0:LANES] = re
                u[k, rows, LANES:W] = im

        @pl.loop(0, F)
        def _(k):
            cos, sin = square_tables(t_ref, k, C)
            part = halves(u[k])
            p = exact_dot(cos, part, ((1,), (0,)))
            q = exact_dot(sin, part, ((1,), (0,)))
            spec_re = p[:, 0:LANES] - q[:, LANES:]
            spec_im = p[:, LANES:] + q[:, 0:LANES]
            lines = pl.ds(k, A, stride=F)
            weight = wf[c, lines, :]
            res_re = weight * spec_re - mf[c, 0, lines, :]
            res_im = weight * spec_im - mf[c, 1, lines, :]
            part = halves(jnp.concatenate([res_re, res_im], axis=1))
            p = exact_dot(cos, part, ((0,), (0,)))
            q = exact_dot(sin, part, ((0,), (0,)))
            u[k, :, 0:LANES] = p[:, 0:LANES] + q[:, LANES:]
            u[k, :, LANES:W] = p[:, LANES:] - q[:, 0:LANES]

        for i, (start, size) in enumerate(pieces if c == C - 1 else [(0, R)]):

            @pl.loop(0, size // 8)
            def _(t):
                rows = pl.ds(pl.multiple_of(start + t * 8, 8), 8)
                values = [(u[k, rows, 0:LANES], u[k, rows, LANES:W]) for k in range(F)]
                for q, (re, im) in enumerate(block_dft(values, 1.0)):
                    sendy[q, rows, c * W:c * W + LANES] = re
                    sendy[q, rows, c * W + LANES:(c + 1) * W] = im

            span = pl.ds(start, size)
            for o in order:
                d = lax.rem(me + o, F)
                copy = pltpu.make_async_remote_copy(
                    src_ref=sendy.at[d, span, wide], dst_ref=recvy.at[me, span, wide],
                    send_sem=bs.at[c, i, o], recv_sem=br.at[c, i, o],
                    device_id={"facet": d}, device_id_type=pl.DeviceIdType.MESH,
                )
                copy.start()
                back[i].append(copy)
            copy = pltpu.make_async_copy(
                sendy.at[me, span, wide], recvy.at[me, span, wide], br.at[c, i, 0]
            )
            copy.start()
            back[i].append(copy)

        if c == 0:
            for copy in image_copies + halos:
                copy.wait()
            for k in range(CH):
                first_up = jnp.where(me > 0, up_ref[k:k + 1, 0:LANES], 0.0)
                first_left = jnp.where(mine > 0, left_ref[k], 0.0)[:, LANES - 1:LANES]
                p = dual[k, 0, :, 0:LANES].astype(jnp.float32)
                q = dual[k, 1, :, 0:LANES].astype(jnp.float32)
                row = lax.broadcasted_iota(jnp.int32, (R, LANES), 0)
                p_prev = jnp.where(row == 0, first_up, pltpu.roll(p, 1, 0))
                right[k] = image_ref[k, 0:R, 0:LANES] - (p_prev - p + first_left - q)
            edges = [halo_copy(right, right_ref, hs.at[3], hr.at[3], {"chan": before})]
            for copy in edges:
                copy.start()

    row = lax.broadcasted_iota(jnp.int32, (BLOCK, T), 0)
    lane = lax.broadcasted_iota(jnp.int32, (BLOCK, T), 1)

    def primal(first, end):
        @pl.loop(first, end)
        def _(at):
            rows = pl.ds(pl.multiple_of(at * BLOCK, BLOCK), BLOCK)
            ahead = pl.ds(pl.multiple_of(jnp.maximum(at - 1, 0) * BLOCK, BLOCK), BLOCK)
            for k in range(CH):
                p = dual[k, 0, rows, :].astype(jnp.float32)
                q = dual[k, 1, rows, :].astype(jnp.float32)
                top = dual[k, 0, ahead, :].astype(jnp.float32)[BLOCK - 1:BLOCK, :]
                top = jnp.where(at > 0, top, jnp.where(me > 0, up_ref[k:k + 1, :], 0.0))
                p_prev = jnp.where(row == 0, top, pltpu.roll(p, 1, 0))
                start = jnp.where(mine > 0, left_ref[k, rows, :], 0.0)[:, LANES - 1:LANES]
                q_prev = jnp.where(lane == 0, start, pltpu.roll(q, 1, 1))
                adjoint = p_prev - p + q_prev - q
                x = image_ref[k, rows, :]
                value = x - step_primal * (grad_ref[k, rows, :] + adjoint)
                grad_ref[k, rows, :] = value
                image_ref[k, rows, :] = 2.0 * value - x

    def shrink(first, end):
        @pl.loop(first, end)
        def _(at):
            rows = pl.ds(pl.multiple_of(at * BLOCK, BLOCK), BLOCK)
            later = pl.ds(pl.multiple_of(at * BLOCK + BLOCK, BLOCK), 8)
            total = jnp.zeros((BLOCK, T), jnp.float32)
            for k in range(CH):
                e = image_ref[k, rows, :]
                following = image_ref[k, later, :][0:1, :]
                down = jnp.where(row == BLOCK - 1, following, pltpu.roll(e, BLOCK - 1, 0)) - e
                side = right_ref[k, rows, :][:, 0:1] - column[rows, :][:, k:k + 1]
                side = jnp.where(mine < CH - 1, side, 0.0)
                over = jnp.where(lane == T - 1, side, pltpu.roll(e, T - 1, 1)) - e
                first_part = dual[k, 0, rows, :].astype(jnp.float32) + step_dual * down
                second_part = dual[k, 1, rows, :].astype(jnp.float32) + step_dual * over
                parts[k, 0] = first_part
                parts[k, 1] = second_part
                total = total + (first_part * first_part + second_part * second_part)
            factor = 1.0 / jnp.maximum(1.0, jnp.sqrt(total) / clip_radius)
            for k in range(CH):
                dual[k, 0, rows, :] = (parts[k, 0] * factor).astype(jnp.bfloat16)
                dual[k, 1, rows, :] = (parts[k, 1] * factor).astype(jnp.bfloat16)

    last = [[] for _ in pieces]

    def finish(h):
        start, size = pieces[h]
        for copy in last[h]:
            copy.wait()
        if h == 0:
            for copy in edges:
                copy.wait()
        tile = jnp.concatenate([edge_ref[k, h, 0:1, :] for k in range(CH)], axis=0)
        tile = jnp.concatenate([tile] * (LANES // CH), axis=0)
        column[start:start + size, :] = tile.T[0:size, :]
        primal(start // BLOCK, (start + size) // BLOCK)
        if h == 0:
            for k in range(CH):
                low[k:k + 1, :] = image_ref[k, 0:8, :][0:1, :]
            copy = halo_copy(low, low_ref, hs.at[2], hr.at[2], {"facet": above})
            copy.start()
            edges.append(copy)
        final = h == len(pieces) - 1
        if final:
            edges[-1].wait()
            for k in range(CH):
                image_ref[k, R:R + 1, :] = jnp.where(me < F - 1, low_ref[k:k + 1, :], 0.0)
        first = max(start // BLOCK - 1, 0)
        end = (start + size) // BLOCK - (0 if final else 1)
        shrink(first, end)

    for h, (start, size) in enumerate(pieces):
        for copy in back[h]:
            copy.wait()

        @pl.loop(0, size // 8)
        def _(t):
            rows = pl.ds(pl.multiple_of(start + t * 8, 8), 8)
            target = pl.ds(pl.multiple_of(t * 8, 8), 8)
            for c in range(C):
                re_at, im_at = pl.ds(c * W, LANES), pl.ds(c * W + LANES, LANES)
                values = [(recvy[j, rows, re_at], recvy[j, rows, im_at]) for j in range(F)]
                for b, (re, im) in enumerate(block_dft(values, 1.0)):
                    z[b, target, re_at] = re
                    z[b, target, im_at] = im

        span = pl.ds(start, size)

        @pl.loop(0, F)
        def _(b):
            line = exact_dot((t_ref[0, b], t_ref[1, b]), halves(z[b]), ((1,), (1,)))
            gt[pl.ds(b, A, stride=F), :] = line * scale

        for e in range(CH):
            edge[h, e] = gt[e * T:e * T + 8, :]
        for j in range(N // LANES):
            g[span, j * LANES:(j + 1) * LANES] = gt[j * LANES:(j + 1) * LANES, :].T[0:size, :]
        for o in range(1, CH):
            d = lax.rem(mine + o, CH)
            last[h].append(pltpu.make_async_remote_copy(
                src_ref=g.at[span, pl.ds(pl.multiple_of(d * T, LANES), T)],
                dst_ref=grad_ref.at[mine, span],
                send_sem=cs.at[h, o], recv_sem=cr.at[h, o],
                device_id={"chan": d}, device_id_type=pl.DeviceIdType.MESH,
            ))
            last[h].append(halo_copy(
                edge.at[h, lax.rem(mine + o + 1, CH)], edge_ref.at[mine, h],
                rs.at[h, o], rr.at[h, o], {"chan": d},
            ))
        last[h].append(pltpu.make_async_copy(
            g.at[span, pl.ds(pl.multiple_of(mine * T, LANES), T)],
            grad_ref.at[mine, span], ls.at[1 + h],
        ))
        last[h].append(pltpu.make_async_copy(
            edge.at[h, after], edge_ref.at[mine, h], rr.at[h, 0]
        ))
        for copy in last[h]:
            copy.start()
        if h >= 2:
            finish(h - 2)
    for h in range(max(len(pieces) - 2, 0), len(pieces)):
        finish(h)


def place(image, dual, image_out, dual_out, sem):
    copies = [
        pltpu.make_async_copy(image, image_out, sem.at[0]),
        pltpu.make_async_copy(dual, dual_out, sem.at[1]),
    ]
    for copy in copies:
        copy.start()
    for copy in copies:
        copy.wait()


def shards(image, weights, measured, dual):
    F, CH = lax.axis_size("facet"), lax.axis_size("chan")
    R, N = image.shape[1:]
    A = N // F
    C = A // LANES
    RC = R // LANES
    seed, turn, table = (jnp.asarray(t) for t in table_seeds(F, A))
    PC = len(back_pieces(R))
    T = N // CH
    HR = -(-CH // 8) * 8
    f32 = jnp.float32
    dma = pltpu.SemaphoreType.DMA
    vmem = pl.BlockSpec(memory_space=pltpu.VMEM)
    hbm = pl.BlockSpec(memory_space=pl.ANY)
    main = pl.BlockSpec(memory_space=pltpu.HBM)
    staged = pl.pallas_call(
        partial(kernel, F, CH),
        out_shape=(
            pltpu.VMEM((CH, R, T), f32),
            pltpu.VMEM((CH, 2, R, T), jnp.bfloat16),
        ),
        in_specs=[main, vmem, vmem, main, main, main, main],
        out_specs=(vmem, vmem),
        scratch_shapes=[
            pltpu.VMEM((2, F, A, 2 * A), jnp.bfloat16),
            pltpu.VMEM((R, N), f32),
            pltpu.VMEM((CH, R + 8, T), f32),
            pltpu.VMEM((HR, T), f32),
            pltpu.VMEM((HR, T), f32),
            pltpu.VMEM((HR, T), f32),
            pltpu.VMEM((HR, T), f32),
            pltpu.VMEM((CH, R, LANES), f32),
            pltpu.VMEM((CH, R, LANES), f32),
            pltpu.VMEM((CH, R, LANES), f32),
            pltpu.VMEM((CH, R, LANES), f32),
            pltpu.VMEM((PC, CH, 8, LANES), f32),
            pltpu.VMEM((CH, PC, 8, LANES), f32),
            pltpu.VMEM((R, LANES), f32),
            pltpu.VMEM((CH, 2, BLOCK, T), f32),
            pltpu.VMEM((RC, N, LANES), f32),
            pltpu.VMEM((F, LANES, 2 * A), f32),
            pltpu.VMEM((C, F, R, 2 * LANES), f32),
            pltpu.VMEM((C, F, R, 2 * LANES), f32),
            pltpu.VMEM((N, A), jnp.bfloat16),
            pltpu.VMEM((2, N, A), jnp.bfloat16),
            pltpu.VMEM((C, N, LANES), f32),
            pltpu.VMEM((C, 2, N, LANES), f32),
            pltpu.VMEM((F, A, 2 * LANES), f32),
            pltpu.VMEM((F, R, 2 * A), f32),
            pltpu.VMEM((F, R, 2 * A), f32),
            pltpu.VMEM((N, LANES), f32),
            pltpu.VMEM((R, N), f32),
            dma((7 + RC,)),
            dma((C, RC, F)), dma((C, RC, F)),
            dma((C, PC, F)), dma((C, PC, F)),
            dma((PC, CH)), dma((PC, CH)),
            dma((CH,)), dma((CH,)),
            dma((1 + PC,)),
            dma((4,)), dma((4,)),
            dma((PC, CH)), dma((PC, CH)),
        ],
        compiler_params=pltpu.CompilerParams(
            collective_id=0, has_side_effects=True, vmem_limit_bytes=54 * 1024 * 1024
        ),
    )(image[0], seed, turn, table, weights, measured, dual)
    return pl.pallas_call(
        place,
        out_shape=tuple(jax.ShapeDtypeStruct(a.shape, a.dtype) for a in staged),
        in_specs=[hbm, hbm],
        out_specs=(hbm, hbm),
        scratch_shapes=[dma((2,))],
        compiler_params=pltpu.CompilerParams(vmem_limit_bytes=2 * 1024 * 1024),
    )(*staged)


def solution(mesh):
    placed = (
        P("chan", "facet", None),
        P("chan", None, "facet"),
        P("chan", None, None, "facet"),
        P(None, None, "facet", "chan"),
    )
    return jax.shard_map(
        shards,
        mesh=mesh,
        in_specs=placed,
        out_specs=(P(None, "facet", "chan"), P(None, None, "facet", "chan")),
        check_vma=False,
    )
```

```python
from functools import partial
import math

import jax
import jax.numpy as jnp
import numpy as np
from jax import lax
from jax.experimental import pallas as pl
from jax.experimental.pallas import tpu as pltpu
from jax.sharding import PartitionSpec as P

step_primal = 0.5
step_dual = 0.5
clip_radius = 4.0
LANES = 128
BLOCK = 16


def turned(real, imag, num, den, sign):
    num = num % den
    if num == 0:
        return real, imag
    if 4 * num == den:
        return (-imag, real) if sign > 0 else (imag, -real)
    c = math.cos(2.0 * math.pi * num / den)
    s = sign * math.sin(2.0 * math.pi * num / den)
    if 8 * num == den:
        h = math.sqrt(0.5)
        if sign > 0:
            return (real - imag) * h, (real + imag) * h
        return (real + imag) * h, (imag - real) * h
    return real * c - imag * s, real * s + imag * c


def block_dft(values, sign):
    n = len(values)
    if n == 1:
        return values
    even = block_dft(values[0::2], sign)
    odd = block_dft(values[1::2], sign)
    low, high = [], []
    for k in range(n // 2):
        er, ei = even[k]
        tr, ti = turned(*odd[k], k, n, sign)
        low.append((er + tr, ei + ti))
        high.append((er - tr, ei - ti))
    return low + high


def halves(x):
    high = x.astype(jnp.bfloat16)
    return high, (x - high.astype(jnp.float32)).astype(jnp.bfloat16)


def exact_dot(first, second, dims):
    (fh, fl), (sh, sl) = first, second
    dot = partial(
        lax.dot_general, dimension_numbers=(dims, ((), ())), preferred_element_type=jnp.float32
    )
    return dot(fh, sh) + (dot(fh, sl) + dot(fl, sh))


def table_seeds(blocks, inner):
    n = blocks * inner
    a = np.arange(max(blocks, inner))[:, None]
    i = np.arange(inner)[None, :]

    def pairs(step, count):
        phase = 2.0 * np.pi / n * ((step * a[:count] * i) % n)
        pair = np.stack([np.cos(phase), -np.sin(phase)], axis=1).astype(np.float32)
        pair = pair.reshape(count, 2, inner // LANES, LANES)
        return pair.transpose(0, 2, 1, 3).reshape(count, 2 * inner)

    phase = 2.0 * np.pi / n * ((blocks * a[None, :inner] + a[:blocks, None]) * i[:, :LANES] % n)
    value = np.concatenate([np.cos(phase), -np.sin(phase)], axis=2).astype(np.float32)
    high = value.astype(jnp.bfloat16)
    low = (value - high.astype(np.float32)).astype(jnp.bfloat16)
    return pairs(blocks, inner), np.repeat(pairs(1, blocks)[:, None, :], 8, axis=1), np.stack([high, low])


def fill_tables(seed_ref, turn_ref, t_ref):
    _, F, A, width = t_ref.shape

    @pl.loop(0, F)
    def _(b):
        for c in range(1, width // (2 * LANES)):
            re_at = slice(2 * c * LANES, (2 * c + 1) * LANES)
            im_at = slice((2 * c + 1) * LANES, (2 * c + 2) * LANES)
            turn_re, turn_im = turn_ref[b, 0:1, re_at], turn_ref[b, 0:1, im_at]

            @pl.loop(0, A // 32)
            def _(t):
                rows = pl.ds(pl.multiple_of(t * 32, 32), 32)
                re, im = seed_ref[rows, re_at], seed_ref[rows, im_at]
                pair = (re * turn_re - im * turn_im, re * turn_im + im * turn_re)
                for value, at in zip(pair, (re_at, im_at)):
                    high, low = halves(value)
                    t_ref[0, b, rows, at] = high
                    t_ref[1, b, rows, at] = low


def back_pieces(rows):
    pieces, start = [], 0
    while rows - start > 2 * BLOCK:
        size = (rows - start) // 2
        pieces.append((start, size))
        start += size
    return pieces + [(start, rows - start)]


def square_tables(t_ref, k, chunks):
    found = []
    for at in (0, LANES):
        pieces = [
            [t_ref[s, k, :, 2 * LANES * c + at:2 * LANES * c + at + LANES] for c in range(chunks)]
            for s in (0, 1)
        ]
        found.append(tuple(jnp.concatenate(p, axis=1) if chunks > 1 else p[0] for p in pieces))
    return found


def halo_copy(source, target, send_sem, recv_sem, device):
    return pltpu.make_async_remote_copy(
        src_ref=source, dst_ref=target, send_sem=send_sem, recv_sem=recv_sem,
        device_id=device, device_id_type=pl.DeviceIdType.MESH,
    )


def kernel(
    F, CH, x_hbm, seed_ref, turn_ref, table_hbm, w_hbm, m_hbm, d_hbm,
    grad_ref, dual,
    t_ref, x_ref, image_ref, up, up_ref, low, low_ref,
    left, left_ref, right, right_ref, edge, edge_ref, column, parts,
    xt, z, send, recv, wb, mb, wf, mf, u, sendy, recvy, gt, g,
    in_sem, fs, fr, bs, br, cs, cr, xs, xr, ls, hs, hr, rs, rr,
):
    R, N = x_ref.shape
    A = N // F
    C = A // LANES
    T = N // CH
    RC = R // LANES
    W = 2 * LANES
    scale = 1.0 / N
    me = lax.axis_index("facet")
    mine = lax.axis_index("chan")
    order = sorted(range(1, F), key=lambda o: abs(o - F // 2))

    load_x = [
        pltpu.make_async_copy(
            x_hbm.at[h * LANES:(h + 1) * LANES], x_ref.at[h * LANES:(h + 1) * LANES],
            in_sem.at[6 + h],
        )
        for h in range(RC)
    ]
    load_t = pltpu.make_async_copy(table_hbm, t_ref.at[:, :, :, 0:W], in_sem.at[6 + RC])
    load_x[0].start()
    load_t.start()
    for copy in load_x[1:]:
        copy.start()
    load_w = pltpu.make_async_copy(w_hbm.at[0], wb, in_sem.at[0])
    load_m = pltpu.make_async_copy(m_hbm.at[0], mb, in_sem.at[1])
    load_w.start()
    load_m.start()
    load_d = pltpu.make_async_copy(d_hbm, dual, in_sem.at[2])
    load_d.start()
    above, below = lax.rem(me + F - 1, F), lax.rem(me + 1, F)
    before, after = lax.rem(mine + CH - 1, CH), lax.rem(mine + 1, CH)

    barrier = pltpu.get_barrier_semaphore()
    for o in range(1, F):
        pl.semaphore_signal(
            barrier, inc=1, device_id={"facet": lax.rem(me + o, F)},
            device_id_type=pl.DeviceIdType.MESH,
        )
    for o in range(1, CH):
        pl.semaphore_signal(
            barrier, inc=1, device_id={"chan": lax.rem(mine + o, CH)},
            device_id_type=pl.DeviceIdType.MESH,
        )

    copies = []
    for c in range(C):
        wide = slice(c * W, (c + 1) * W)
        group = []
        for h in range(RC):
            if c == 0:
                load_x[h].wait()
                for j in range(N // LANES):
                    xt[h, j * LANES:(j + 1) * LANES, :] = x_ref[
                        h * LANES:(h + 1) * LANES, j * LANES:(j + 1) * LANES
                    ].T

            if c == 0 and h == 0:
                load_t.wait()

            @pl.loop(0, F)
            def _(b):
                part = halves(xt[h, pl.ds(b, A, stride=F), :].T)
                table = (t_ref[0, b, :, wide], t_ref[1, b, :, wide])
                z[b, 0:LANES, 0:W] = exact_dot(part, table, ((1,), (0,)))

            @pl.loop(0, LANES // 8)
            def _(t):
                rows = pl.ds(pl.multiple_of(t * 8, 8), 8)
                target = pl.ds(pl.multiple_of(h * LANES + t * 8, 8), 8)
                values = [(z[b, rows, 0:LANES], z[b, rows, LANES:W]) for b in range(F)]
                for j, (re, im) in enumerate(block_dft(values, -1.0)):
                    send[c, j, target, 0:LANES] = re
                    send[c, j, target, LANES:W] = im

            if c == 0 and h == 0:
                pl.semaphore_wait(barrier, F - 1 + CH - 1)
            span = pl.ds(h * LANES, LANES)
            for o in order:
                d = lax.rem(me + o, F)
                copy = pltpu.make_async_remote_copy(
                    src_ref=send.at[c, d, span], dst_ref=recv.at[c, me, span],
                    send_sem=fs.at[c, h, o], recv_sem=fr.at[c, h, o],
                    device_id={"facet": d}, device_id_type=pl.DeviceIdType.MESH,
                )
                copy.start()
                group.append(copy)
            copy = pltpu.make_async_copy(
                send.at[c, me, span], recv.at[c, me, span], fr.at[c, h, 0]
            )
            copy.start()
            group.append(copy)
        copies.append(group)
        if c == 0:
            fill_tables(seed_ref, turn_ref, t_ref)
            load_d.wait()
            for k in range(CH):
                up[k:k + 1, :] = dual[k, 0, R - 16:R, :].astype(jnp.float32)[15:16, :]
                left[k] = dual[k, 1, :, T - LANES:T].astype(jnp.float32)
            halos = [
                halo_copy(up, up_ref, hs.at[0], hr.at[0], {"facet": below}),
                halo_copy(left, left_ref, hs.at[1], hr.at[1], {"chan": after}),
            ]
            for copy in halos:
                copy.start()

            image_copies = []
            for o in range(1, CH):
                d = lax.rem(mine + o, CH)
                copy = pltpu.make_async_remote_copy(
                    src_ref=x_ref.at[:, pl.ds(pl.multiple_of(d * T, LANES), T)],
                    dst_ref=image_ref.at[mine, 0:R],
                    send_sem=xs.at[o], recv_sem=xr.at[o],
                    device_id={"chan": d}, device_id_type=pl.DeviceIdType.MESH,
                )
                copy.start()
                image_copies.append(copy)
            own = pltpu.make_async_copy(
                x_ref.at[:, pl.ds(pl.multiple_of(mine * T, LANES), T)], image_ref.at[mine, 0:R], ls.at[0]
            )
            own.start()
            image_copies.append(own)

    load_w.wait()
    load_m.wait()

    @pl.loop(0, N // 16)
    def _(t):
        rows = pl.ds(pl.multiple_of(t * 16, 16), 16)
        for c in range(C):
            lo = c * LANES
            wf[c, rows, :] = wb[rows, lo:lo + LANES].astype(jnp.float32) * scale
            mf[c, 0, rows, :] = mb[0, rows, lo:lo + LANES].astype(jnp.float32)
            mf[c, 1, rows, :] = mb[1, rows, lo:lo + LANES].astype(jnp.float32)

    pieces = back_pieces(R)
    back = [[] for _ in pieces]
    for c in range(C):
        wide = slice(c * W, (c + 1) * W)
        for copy in copies[c]:
            copy.wait()

        @pl.loop(0, R // 8)
        def _(t):
            rows = pl.ds(pl.multiple_of(t * 8, 8), 8)
            values = [(recv[c, q, rows, 0:LANES], recv[c, q, rows, LANES:W]) for q in range(F)]
            for k, (re, im) in enumerate(block_dft(values, -1.0)):
                u[k, rows, 0:LANES] = re
                u[k, rows, LANES:W] = im

        @pl.loop(0, F)
        def _(k):
            cos, sin = square_tables(t_ref, k, C)
            part = halves(u[k])
            p = exact_dot(cos, part, ((1,), (0,)))
            q = exact_dot(sin, part, ((1,), (0,)))
            spec_re = p[:, 0:LANES] - q[:, LANES:]
            spec_im = p[:, LANES:] + q[:, 0:LANES]
            lines = pl.ds(k, A, stride=F)
            weight = wf[c, lines, :]
            res_re = weight * spec_re - mf[c, 0, lines, :]
            res_im = weight * spec_im - mf[c, 1, lines, :]
            part = halves(jnp.concatenate([res_re, res_im], axis=1))
            p = exact_dot(cos, part, ((0,), (0,)))
            q = exact_dot(sin, part, ((0,), (0,)))
            u[k, :, 0:LANES] = p[:, 0:LANES] + q[:, LANES:]
            u[k, :, LANES:W] = p[:, LANES:] - q[:, 0:LANES]

        @pl.loop(0, R // 8)
        def _(t):
            rows = pl.ds(pl.multiple_of(t * 8, 8), 8)
            values = [(u[k, rows, 0:LANES], u[k, rows, LANES:W]) for k in range(F)]
            for q, (re, im) in enumerate(block_dft(values, 1.0)):
                sendy[q, rows, c * W:c * W + LANES] = re
                sendy[q, rows, c * W + LANES:(c + 1) * W] = im

        parcels = [(0, pieces[0], wide)]
        if c == C - 1:
            parcels += [(i, piece, slice(0, C * W)) for i, piece in enumerate(pieces) if i > 0]
        for i, (start, size), across in parcels:
            span = pl.ds(start, size)
            for o in order:
                d = lax.rem(me + o, F)
                copy = pltpu.make_async_remote_copy(
                    src_ref=sendy.at[d, span, across], dst_ref=recvy.at[me, span, across],
                    send_sem=bs.at[c, i, o], recv_sem=br.at[c, i, o],
                    device_id={"facet": d}, device_id_type=pl.DeviceIdType.MESH,
                )
                copy.start()
                back[i].append(copy)
            copy = pltpu.make_async_copy(
                sendy.at[me, span, across], recvy.at[me, span, across], br.at[c, i, 0]
            )
            copy.start()
            back[i].append(copy)

        if c == 0:
            for copy in image_copies + halos:
                copy.wait()
            for k in range(CH):
                first_up = jnp.where(me > 0, up_ref[k:k + 1, 0:LANES], 0.0)
                first_left = jnp.where(mine > 0, left_ref[k], 0.0)[:, LANES - 1:LANES]
                p = dual[k, 0, :, 0:LANES].astype(jnp.float32)
                q = dual[k, 1, :, 0:LANES].astype(jnp.float32)
                row = lax.broadcasted_iota(jnp.int32, (R, LANES), 0)
                p_prev = jnp.where(row == 0, first_up, pltpu.roll(p, 1, 0))
                right[k] = image_ref[k, 0:R, 0:LANES] - (p_prev - p + first_left - q)
            edges = [halo_copy(right, right_ref, hs.at[3], hr.at[3], {"chan": before})]
            for copy in edges:
                copy.start()

    row = lax.broadcasted_iota(jnp.int32, (BLOCK, T), 0)
    lane = lax.broadcasted_iota(jnp.int32, (BLOCK, T), 1)

    def primal(first, end):
        @pl.loop(first, end)
        def _(at):
            rows = pl.ds(pl.multiple_of(at * BLOCK, BLOCK), BLOCK)
            ahead = pl.ds(pl.multiple_of(jnp.maximum(at - 1, 0) * BLOCK, BLOCK), BLOCK)
            for k in range(CH):
                p = dual[k, 0, rows, :].astype(jnp.float32)
                q = dual[k, 1, rows, :].astype(jnp.float32)
                top = dual[k, 0, ahead, :].astype(jnp.float32)[BLOCK - 1:BLOCK, :]
                top = jnp.where(at > 0, top, jnp.where(me > 0, up_ref[k:k + 1, :], 0.0))
                p_prev = jnp.where(row == 0, top, pltpu.roll(p, 1, 0))
                start = jnp.where(mine > 0, left_ref[k, rows, :], 0.0)[:, LANES - 1:LANES]
                q_prev = jnp.where(lane == 0, start, pltpu.roll(q, 1, 1))
                adjoint = p_prev - p + q_prev - q
                x = image_ref[k, rows, :]
                value = x - step_primal * (grad_ref[k, rows, :] + adjoint)
                grad_ref[k, rows, :] = value
                image_ref[k, rows, :] = 2.0 * value - x

    def shrink(first, end):
        @pl.loop(first, end)
        def _(at):
            rows = pl.ds(pl.multiple_of(at * BLOCK, BLOCK), BLOCK)
            later = pl.ds(pl.multiple_of(at * BLOCK + BLOCK, BLOCK), 8)
            total = jnp.zeros((BLOCK, T), jnp.float32)
            for k in range(CH):
                e = image_ref[k, rows, :]
                following = image_ref[k, later, :][0:1, :]
                down = jnp.where(row == BLOCK - 1, following, pltpu.roll(e, BLOCK - 1, 0)) - e
                side = right_ref[k, rows, :][:, 0:1] - column[rows, :][:, k:k + 1]
                side = jnp.where(mine < CH - 1, side, 0.0)
                over = jnp.where(lane == T - 1, side, pltpu.roll(e, T - 1, 1)) - e
                first_part = dual[k, 0, rows, :].astype(jnp.float32) + step_dual * down
                second_part = dual[k, 1, rows, :].astype(jnp.float32) + step_dual * over
                parts[k, 0] = first_part
                parts[k, 1] = second_part
                total = total + (first_part * first_part + second_part * second_part)
            factor = 1.0 / jnp.maximum(1.0, jnp.sqrt(total) / clip_radius)
            for k in range(CH):
                dual[k, 0, rows, :] = (parts[k, 0] * factor).astype(jnp.bfloat16)
                dual[k, 1, rows, :] = (parts[k, 1] * factor).astype(jnp.bfloat16)

    last = [[] for _ in pieces]

    def finish(h):
        start, size = pieces[h]
        for copy in last[h]:
            copy.wait()
        if h == 0:
            for copy in edges:
                copy.wait()
        tile = jnp.concatenate([edge_ref[k, h, 0:1, :] for k in range(CH)], axis=0)
        tile = jnp.concatenate([tile] * (LANES // CH), axis=0)
        column[start:start + size, :] = tile.T[0:size, :]
        primal(start // BLOCK, (start + size) // BLOCK)
        if h == 0:
            for k in range(CH):
                low[k:k + 1, :] = image_ref[k, 0:8, :][0:1, :]
            copy = halo_copy(low, low_ref, hs.at[2], hr.at[2], {"facet": above})
            copy.start()
            edges.append(copy)
        final = h == len(pieces) - 1
        if final:
            edges[-1].wait()
            for k in range(CH):
                image_ref[k, R:R + 1, :] = jnp.where(me < F - 1, low_ref[k:k + 1, :], 0.0)
        first = max(start // BLOCK - 1, 0)
        end = (start + size) // BLOCK - (0 if final else 1)
        shrink(first, end)

    for h, (start, size) in enumerate(pieces):
        for copy in back[h]:
            copy.wait()

        @pl.loop(0, size // 8)
        def _(t):
            rows = pl.ds(pl.multiple_of(start + t * 8, 8), 8)
            target = pl.ds(pl.multiple_of(t * 8, 8), 8)
            for c in range(C):
                re_at, im_at = pl.ds(c * W, LANES), pl.ds(c * W + LANES, LANES)
                values = [(recvy[j, rows, re_at], recvy[j, rows, im_at]) for j in range(F)]
                for b, (re, im) in enumerate(block_dft(values, 1.0)):
                    z[b, target, re_at] = re
                    z[b, target, im_at] = im

        span = pl.ds(start, size)

        @pl.loop(0, F, unroll=F)
        def _(b):
            line = exact_dot((t_ref[0, b], t_ref[1, b]), halves(z[b]), ((1,), (1,)))
            gt[pl.ds(b, A, stride=F), :] = line * scale

        for e in range(CH):
            edge[h, e] = gt[e * T:e * T + 8, :]
        for j in range(N // LANES):
            g[span, j * LANES:(j + 1) * LANES] = gt[j * LANES:(j + 1) * LANES, :].T[0:size, :]
        for o in range(1, CH):
            d = lax.rem(mine + o, CH)
            last[h].append(pltpu.make_async_remote_copy(
                src_ref=g.at[span, pl.ds(pl.multiple_of(d * T, LANES), T)],
                dst_ref=grad_ref.at[mine, span],
                send_sem=cs.at[h, o], recv_sem=cr.at[h, o],
                device_id={"chan": d}, device_id_type=pl.DeviceIdType.MESH,
            ))
            last[h].append(halo_copy(
                edge.at[h, lax.rem(mine + o + 1, CH)], edge_ref.at[mine, h],
                rs.at[h, o], rr.at[h, o], {"chan": d},
            ))
        last[h].append(pltpu.make_async_copy(
            g.at[span, pl.ds(pl.multiple_of(mine * T, LANES), T)],
            grad_ref.at[mine, span], ls.at[1 + h],
        ))
        last[h].append(pltpu.make_async_copy(
            edge.at[h, after], edge_ref.at[mine, h], rr.at[h, 0]
        ))
        for copy in last[h]:
            copy.start()
        if h >= 2:
            finish(h - 2)
    for h in range(max(len(pieces) - 2, 0), len(pieces)):
        finish(h)


def place(image, dual, image_out, dual_out, sem):
    copies = [
        pltpu.make_async_copy(image, image_out, sem.at[0]),
        pltpu.make_async_copy(dual, dual_out, sem.at[1]),
    ]
    for copy in copies:
        copy.start()
    for copy in copies:
        copy.wait()


def shards(image, weights, measured, dual):
    F, CH = lax.axis_size("facet"), lax.axis_size("chan")
    R, N = image.shape[1:]
    A = N // F
    C = A // LANES
    RC = R // LANES
    seed, turn, table = (jnp.asarray(t) for t in table_seeds(F, A))
    PC = len(back_pieces(R))
    T = N // CH
    HR = -(-CH // 8) * 8
    f32 = jnp.float32
    dma = pltpu.SemaphoreType.DMA
    vmem = pl.BlockSpec(memory_space=pltpu.VMEM)
    hbm = pl.BlockSpec(memory_space=pl.ANY)
    main = pl.BlockSpec(memory_space=pltpu.HBM)
    staged = pl.pallas_call(
        partial(kernel, F, CH),
        out_shape=(
            pltpu.VMEM((CH, R, T), f32),
            pltpu.VMEM((CH, 2, R, T), jnp.bfloat16),
        ),
        in_specs=[main, vmem, vmem, main, main, main, main],
        out_specs=(vmem, vmem),
        scratch_shapes=[
            pltpu.VMEM((2, F, A, 2 * A), jnp.bfloat16),
            pltpu.VMEM((R, N), f32),
            pltpu.VMEM((CH, R + 8, T), f32),
            pltpu.VMEM((HR, T), f32),
            pltpu.VMEM((HR, T), f32),
            pltpu.VMEM((HR, T), f32),
            pltpu.VMEM((HR, T), f32),
            pltpu.VMEM((CH, R, LANES), f32),
            pltpu.VMEM((CH, R, LANES), f32),
            pltpu.VMEM((CH, R, LANES), f32),
            pltpu.VMEM((CH, R, LANES), f32),
            pltpu.VMEM((PC, CH, 8, LANES), f32),
            pltpu.VMEM((CH, PC, 8, LANES), f32),
            pltpu.VMEM((R, LANES), f32),
            pltpu.VMEM((CH, 2, BLOCK, T), f32),
            pltpu.VMEM((RC, N, LANES), f32),
            pltpu.VMEM((F, LANES, 2 * A), f32),
            pltpu.VMEM((C, F, R, 2 * LANES), f32),
            pltpu.VMEM((C, F, R, 2 * LANES), f32),
            pltpu.VMEM((N, A), jnp.bfloat16),
            pltpu.VMEM((2, N, A), jnp.bfloat16),
            pltpu.VMEM((C, N, LANES), f32),
            pltpu.VMEM((C, 2, N, LANES), f32),
            pltpu.VMEM((F, A, 2 * LANES), f32),
            pltpu.VMEM((F, R, 2 * A), f32),
            pltpu.VMEM((F, R, 2 * A), f32),
            pltpu.VMEM((N, LANES), f32),
            pltpu.VMEM((R, N), f32),
            dma((7 + RC,)),
            dma((C, RC, F)), dma((C, RC, F)),
            dma((C, PC, F)), dma((C, PC, F)),
            dma((PC, CH)), dma((PC, CH)),
            dma((CH,)), dma((CH,)),
            dma((1 + PC,)),
            dma((4,)), dma((4,)),
            dma((PC, CH)), dma((PC, CH)),
        ],
        compiler_params=pltpu.CompilerParams(
            collective_id=0, has_side_effects=True, vmem_limit_bytes=54 * 1024 * 1024
        ),
    )(image[0], seed, turn, table, weights, measured, dual)
    return pl.pallas_call(
        place,
        out_shape=tuple(jax.ShapeDtypeStruct(a.shape, a.dtype) for a in staged),
        in_specs=[hbm, hbm],
        out_specs=(hbm, hbm),
        scratch_shapes=[dma((2,))],
        compiler_params=pltpu.CompilerParams(vmem_limit_bytes=2 * 1024 * 1024),
    )(*staged)


def solution(mesh):
    placed = (
        P("chan", "facet", None),
        P("chan", None, "facet"),
        P("chan", None, None, "facet"),
        P(None, None, "facet", "chan"),
    )
    return jax.shard_map(
        shards,
        mesh=mesh,
        in_specs=placed,
        out_specs=(P(None, "facet", "chan"), P(None, None, "facet", "chan")),
        check_vma=False,
    )
```

```python
from functools import partial
import math

import jax
import jax.numpy as jnp
import numpy as np
from jax import lax
from jax.experimental import pallas as pl
from jax.experimental.pallas import tpu as pltpu
from jax.sharding import PartitionSpec as P

step_primal = 0.5
step_dual = 0.5
clip_radius = 4.0
LANES = 128
BLOCK = 16


def turned(real, imag, num, den, sign):
    num = num % den
    if num == 0:
        return real, imag
    if 4 * num == den:
        return (-imag, real) if sign > 0 else (imag, -real)
    c = math.cos(2.0 * math.pi * num / den)
    s = sign * math.sin(2.0 * math.pi * num / den)
    if 8 * num == den:
        h = math.sqrt(0.5)
        if sign > 0:
            return (real - imag) * h, (real + imag) * h
        return (real + imag) * h, (imag - real) * h
    return real * c - imag * s, real * s + imag * c


def block_dft(values, sign):
    n = len(values)
    if n == 1:
        return values
    even = block_dft(values[0::2], sign)
    odd = block_dft(values[1::2], sign)
    low, high = [], []
    for k in range(n // 2):
        er, ei = even[k]
        tr, ti = turned(*odd[k], k, n, sign)
        low.append((er + tr, ei + ti))
        high.append((er - tr, ei - ti))
    return low + high


def halves(x):
    high = x.astype(jnp.bfloat16)
    return high, (x - high.astype(jnp.float32)).astype(jnp.bfloat16)


def exact_dot(first, second, dims):
    (fh, fl), (sh, sl) = first, second
    dot = partial(
        lax.dot_general, dimension_numbers=(dims, ((), ())), preferred_element_type=jnp.float32
    )
    return dot(fh, sh) + (dot(fh, sl) + dot(fl, sh))


def table_seeds(blocks, inner):
    n = blocks * inner
    a = np.arange(max(blocks, inner))[:, None]
    i = np.arange(inner)[None, :]

    def pairs(step, count):
        phase = 2.0 * np.pi / n * ((step * a[:count] * i) % n)
        pair = np.stack([np.cos(phase), -np.sin(phase)], axis=1).astype(np.float32)
        pair = pair.reshape(count, 2, inner // LANES, LANES)
        return pair.transpose(0, 2, 1, 3).reshape(count, 2 * inner)

    phase = 2.0 * np.pi / n * ((blocks * a[None, :inner] + a[:blocks, None]) * i[:, :LANES] % n)
    value = np.concatenate([np.cos(phase), -np.sin(phase)], axis=2).astype(np.float32)
    high = value.astype(jnp.bfloat16)
    low = (value - high.astype(np.float32)).astype(jnp.bfloat16)
    return pairs(blocks, inner), np.repeat(pairs(1, blocks)[:, None, :], 8, axis=1), np.stack([high, low])


def fill_tables(seed_ref, turn_ref, t_ref):
    _, F, A, width = t_ref.shape

    @pl.loop(0, F)
    def _(b):
        for c in range(1, width // (2 * LANES)):
            re_at = slice(2 * c * LANES, (2 * c + 1) * LANES)
            im_at = slice((2 * c + 1) * LANES, (2 * c + 2) * LANES)
            turn_re, turn_im = turn_ref[b, 0:1, re_at], turn_ref[b, 0:1, im_at]

            @pl.loop(0, A // 32)
            def _(t):
                rows = pl.ds(pl.multiple_of(t * 32, 32), 32)
                re, im = seed_ref[rows, re_at], seed_ref[rows, im_at]
                pair = (re * turn_re - im * turn_im, re * turn_im + im * turn_re)
                for value, at in zip(pair, (re_at, im_at)):
                    high, low = halves(value)
                    t_ref[0, b, rows, at] = high
                    t_ref[1, b, rows, at] = low


def back_pieces(rows):
    pieces, start = [], 0
    while rows - start > 2 * BLOCK:
        size = (rows - start) // 2
        pieces.append((start, size))
        start += size
    return pieces + [(start, rows - start)]


def square_tables(t_ref, k, chunks):
    found = []
    for at in (0, LANES):
        pieces = [
            [t_ref[s, k, :, 2 * LANES * c + at:2 * LANES * c + at + LANES] for c in range(chunks)]
            for s in (0, 1)
        ]
        found.append(tuple(jnp.concatenate(p, axis=1) if chunks > 1 else p[0] for p in pieces))
    return found


def halo_copy(source, target, send_sem, recv_sem, device):
    return pltpu.make_async_remote_copy(
        src_ref=source, dst_ref=target, send_sem=send_sem, recv_sem=recv_sem,
        device_id=device, device_id_type=pl.DeviceIdType.MESH,
    )


def kernel(
    F, CH, x_hbm, seed_ref, turn_ref, table_hbm, w_hbm, m_hbm, d_hbm,
    grad_ref, dual,
    t_ref, x_ref, image_ref, up, up_ref, low, low_ref,
    left, left_ref, right, right_ref, edge, edge_ref, column, parts,
    xt, z, send, recv, wb, mb, wf, mf, u, sendy, recvy, gt, g,
    in_sem, fs, fr, bs, br, cs, cr, xs, xr, ls, hs, hr, rs, rr,
):
    R, N = x_ref.shape
    A = N // F
    C = A // LANES
    T = N // CH
    RC = R // LANES
    W = 2 * LANES
    scale = 1.0 / N
    me = lax.axis_index("facet")
    mine = lax.axis_index("chan")
    order = sorted(range(1, F), key=lambda o: abs(o - F // 2))

    load_x = [
        pltpu.make_async_copy(
            x_hbm.at[h * LANES:(h + 1) * LANES], x_ref.at[h * LANES:(h + 1) * LANES],
            in_sem.at[6 + h],
        )
        for h in range(RC)
    ]
    load_t = pltpu.make_async_copy(table_hbm, t_ref.at[:, :, :, 0:W], in_sem.at[6 + RC])
    load_x[0].start()
    load_t.start()
    for copy in load_x[1:]:
        copy.start()
    load_w = pltpu.make_async_copy(w_hbm.at[0], wb, in_sem.at[0])
    load_m = pltpu.make_async_copy(m_hbm.at[0], mb, in_sem.at[1])
    load_w.start()
    load_m.start()
    load_d = pltpu.make_async_copy(d_hbm, dual, in_sem.at[2])
    load_d.start()
    above, below = lax.rem(me + F - 1, F), lax.rem(me + 1, F)
    before, after = lax.rem(mine + CH - 1, CH), lax.rem(mine + 1, CH)

    barrier = pltpu.get_barrier_semaphore()
    for o in range(1, F):
        pl.semaphore_signal(
            barrier, inc=1, device_id={"facet": lax.rem(me + o, F)},
            device_id_type=pl.DeviceIdType.MESH,
        )
    for o in range(1, CH):
        pl.semaphore_signal(
            barrier, inc=1, device_id={"chan": lax.rem(mine + o, CH)},
            device_id_type=pl.DeviceIdType.MESH,
        )

    copies = []
    for c in range(C):
        wide = slice(c * W, (c + 1) * W)
        group = []
        for h in range(RC):
            if c == 0:
                load_x[h].wait()
                for j in range(N // LANES):
                    xt[h, j * LANES:(j + 1) * LANES, :] = x_ref[
                        h * LANES:(h + 1) * LANES, j * LANES:(j + 1) * LANES
                    ].T

            if c == 0 and h == 0:
                load_t.wait()

            @pl.loop(0, F)
            def _(b):
                part = halves(xt[h, pl.ds(b, A, stride=F), :].T)
                table = (t_ref[0, b, :, wide], t_ref[1, b, :, wide])
                z[b, 0:LANES, 0:W] = exact_dot(part, table, ((1,), (0,)))

            @pl.loop(0, LANES // 8)
            def _(t):
                rows = pl.ds(pl.multiple_of(t * 8, 8), 8)
                target = pl.ds(pl.multiple_of(h * LANES + t * 8, 8), 8)
                values = [(z[b, rows, 0:LANES], z[b, rows, LANES:W]) for b in range(F)]
                for j, (re, im) in enumerate(block_dft(values, -1.0)):
                    send[c, j, target, 0:LANES] = re
                    send[c, j, target, LANES:W] = im

            if c == 0 and h == 0:
                pl.semaphore_wait(barrier, F - 1 + CH - 1)
            span = pl.ds(h * LANES, LANES)
            for o in order:
                d = lax.rem(me + o, F)
                copy = pltpu.make_async_remote_copy(
                    src_ref=send.at[c, d, span], dst_ref=recv.at[c, me, span],
                    send_sem=fs.at[c, h, o], recv_sem=fr.at[c, h, o],
                    device_id={"facet": d}, device_id_type=pl.DeviceIdType.MESH,
                )
                copy.start()
                group.append(copy)
            copy = pltpu.make_async_copy(
                send.at[c, me, span], recv.at[c, me, span], fr.at[c, h, 0]
            )
            copy.start()
            group.append(copy)
        copies.append(group)
        if c == 0:
            fill_tables(seed_ref, turn_ref, t_ref)
            load_d.wait()
            for k in range(CH):
                up[k:k + 1, :] = dual[k, 0, R - 16:R, :].astype(jnp.float32)[15:16, :]
                left[k] = dual[k, 1, :, T - LANES:T].astype(jnp.float32)
            halos = [
                halo_copy(up, up_ref, hs.at[0], hr.at[0], {"facet": below}),
                halo_copy(left, left_ref, hs.at[1], hr.at[1], {"chan": after}),
            ]
            for copy in halos:
                copy.start()

            image_copies = []
            for o in range(1, CH):
                d = lax.rem(mine + o, CH)
                copy = pltpu.make_async_remote_copy(
                    src_ref=x_ref.at[:, pl.ds(pl.multiple_of(d * T, LANES), T)],
                    dst_ref=image_ref.at[mine, 0:R],
                    send_sem=xs.at[o], recv_sem=xr.at[o],
                    device_id={"chan": d}, device_id_type=pl.DeviceIdType.MESH,
                )
                copy.start()
                image_copies.append(copy)
            own = pltpu.make_async_copy(
                x_ref.at[:, pl.ds(pl.multiple_of(mine * T, LANES), T)], image_ref.at[mine, 0:R], ls.at[0]
            )
            own.start()
            image_copies.append(own)

    load_w.wait()
    load_m.wait()

    @pl.loop(0, N // 16)
    def _(t):
        rows = pl.ds(pl.multiple_of(t * 16, 16), 16)
        for c in range(C):
            lo = c * LANES
            wf[c, rows, :] = wb[rows, lo:lo + LANES].astype(jnp.float32) * scale
            mf[c, 0, rows, :] = mb[0, rows, lo:lo + LANES].astype(jnp.float32)
            mf[c, 1, rows, :] = mb[1, rows, lo:lo + LANES].astype(jnp.float32)

    pieces = back_pieces(R)
    back = [[] for _ in pieces]
    for c in range(C):
        wide = slice(c * W, (c + 1) * W)
        for copy in copies[c]:
            copy.wait()

        @pl.loop(0, R // 8)
        def _(t):
            rows = pl.ds(pl.multiple_of(t * 8, 8), 8)
            values = [(recv[c, q, rows, 0:LANES], recv[c, q, rows, LANES:W]) for q in range(F)]
            for k, (re, im) in enumerate(block_dft(values, -1.0)):
                u[k, rows, 0:LANES] = re
                u[k, rows, LANES:W] = im

        @pl.loop(0, F)
        def _(k):
            cos, sin = square_tables(t_ref, k, C)
            part = halves(u[k])
            p = exact_dot(cos, part, ((1,), (0,)))
            q = exact_dot(sin, part, ((1,), (0,)))
            spec_re = p[:, 0:LANES] - q[:, LANES:]
            spec_im = p[:, LANES:] + q[:, 0:LANES]
            lines = pl.ds(k, A, stride=F)
            weight = wf[c, lines, :]
            res_re = weight * spec_re - mf[c, 0, lines, :]
            res_im = weight * spec_im - mf[c, 1, lines, :]
            part = halves(jnp.concatenate([res_re, res_im], axis=1))
            p = exact_dot(cos, part, ((0,), (0,)))
            q = exact_dot(sin, part, ((0,), (0,)))
            u[k, :, 0:LANES] = p[:, 0:LANES] + q[:, LANES:]
            u[k, :, LANES:W] = p[:, LANES:] - q[:, 0:LANES]

        @pl.loop(0, R // 8)
        def _(t):
            rows = pl.ds(pl.multiple_of(t * 8, 8), 8)
            values = [(u[k, rows, 0:LANES], u[k, rows, LANES:W]) for k in range(F)]
            for q, (re, im) in enumerate(block_dft(values, 1.0)):
                sendy[q, rows, c * W:c * W + LANES] = re
                sendy[q, rows, c * W + LANES:(c + 1) * W] = im

        parcels = [(0, pieces[0], wide)]
        if c == C - 1:
            parcels += [(i, piece, slice(0, C * W)) for i, piece in enumerate(pieces) if i > 0]
        for i, (start, size), across in parcels:
            span = pl.ds(start, size)
            for o in order:
                d = lax.rem(me + o, F)
                copy = pltpu.make_async_remote_copy(
                    src_ref=sendy.at[d, span, across], dst_ref=recvy.at[me, span, across],
                    send_sem=bs.at[c, i, o], recv_sem=br.at[c, i, o],
                    device_id={"facet": d}, device_id_type=pl.DeviceIdType.MESH,
                )
                copy.start()
                back[i].append(copy)
            copy = pltpu.make_async_copy(
                sendy.at[me, span, across], recvy.at[me, span, across], br.at[c, i, 0]
            )
            copy.start()
            back[i].append(copy)

        if c == 0:
            for copy in image_copies + halos:
                copy.wait()
            for k in range(CH):
                first_up = jnp.where(me > 0, up_ref[k:k + 1, 0:LANES], 0.0)
                first_left = jnp.where(mine > 0, left_ref[k], 0.0)[:, LANES - 1:LANES]
                p = dual[k, 0, :, 0:LANES].astype(jnp.float32)
                q = dual[k, 1, :, 0:LANES].astype(jnp.float32)
                row = lax.broadcasted_iota(jnp.int32, (R, LANES), 0)
                p_prev = jnp.where(row == 0, first_up, pltpu.roll(p, 1, 0))
                right[k] = image_ref[k, 0:R, 0:LANES] - (p_prev - p + first_left - q)
            edges = [halo_copy(right, right_ref, hs.at[3], hr.at[3], {"chan": before})]
            for copy in edges:
                copy.start()

    row = lax.broadcasted_iota(jnp.int32, (BLOCK, T), 0)
    lane = lax.broadcasted_iota(jnp.int32, (BLOCK, T), 1)

    def primal(first, end):
        @pl.loop(first, end, unroll=(end - first) if end - first < 4 else 1)
        def _(at):
            rows = pl.ds(pl.multiple_of(at * BLOCK, BLOCK), BLOCK)
            ahead = pl.ds(pl.multiple_of(jnp.maximum(at - 1, 0) * BLOCK, BLOCK), BLOCK)
            for k in range(CH):
                p = dual[k, 0, rows, :].astype(jnp.float32)
                q = dual[k, 1, rows, :].astype(jnp.float32)
                top = dual[k, 0, ahead, :].astype(jnp.float32)[BLOCK - 1:BLOCK, :]
                top = jnp.where(at > 0, top, jnp.where(me > 0, up_ref[k:k + 1, :], 0.0))
                p_prev = jnp.where(row == 0, top, pltpu.roll(p, 1, 0))
                start = jnp.where(mine > 0, left_ref[k, rows, :], 0.0)[:, LANES - 1:LANES]
                q_prev = jnp.where(lane == 0, start, pltpu.roll(q, 1, 1))
                adjoint = p_prev - p + q_prev - q
                x = image_ref[k, rows, :]
                value = x - step_primal * (grad_ref[k, rows, :] + adjoint)
                grad_ref[k, rows, :] = value
                image_ref[k, rows, :] = 2.0 * value - x

    def shrink(first, end):
        @pl.loop(first, end, unroll=(end - first) if end - first < 4 else 1)
        def _(at):
            rows = pl.ds(pl.multiple_of(at * BLOCK, BLOCK), BLOCK)
            later = pl.ds(pl.multiple_of(at * BLOCK + BLOCK, BLOCK), 8)
            total = jnp.zeros((BLOCK, T), jnp.float32)
            for k in range(CH):
                e = image_ref[k, rows, :]
                following = image_ref[k, later, :][0:1, :]
                down = jnp.where(row == BLOCK - 1, following, pltpu.roll(e, BLOCK - 1, 0)) - e
                side = right_ref[k, rows, :][:, 0:1] - column[rows, :][:, k:k + 1]
                side = jnp.where(mine < CH - 1, side, 0.0)
                over = jnp.where(lane == T - 1, side, pltpu.roll(e, T - 1, 1)) - e
                first_part = dual[k, 0, rows, :].astype(jnp.float32) + step_dual * down
                second_part = dual[k, 1, rows, :].astype(jnp.float32) + step_dual * over
                parts[k, 0] = first_part
                parts[k, 1] = second_part
                total = total + (first_part * first_part + second_part * second_part)
            factor = 1.0 / jnp.maximum(1.0, jnp.sqrt(total) / clip_radius)
            for k in range(CH):
                dual[k, 0, rows, :] = (parts[k, 0] * factor).astype(jnp.bfloat16)
                dual[k, 1, rows, :] = (parts[k, 1] * factor).astype(jnp.bfloat16)

    last = [[] for _ in pieces]

    def finish(h):
        start, size = pieces[h]
        for copy in last[h]:
            copy.wait()
        if h == 0:
            for copy in edges:
                copy.wait()
        tile = jnp.concatenate([edge_ref[k, h, 0:1, :] for k in range(CH)], axis=0)
        tile = jnp.concatenate([tile] * (LANES // CH), axis=0)
        column[start:start + size, :] = tile.T[0:size, :]
        primal(start // BLOCK, (start + size) // BLOCK)
        if h == 0:
            for k in range(CH):
                low[k:k + 1, :] = image_ref[k, 0:8, :][0:1, :]
            copy = halo_copy(low, low_ref, hs.at[2], hr.at[2], {"facet": above})
            copy.start()
            edges.append(copy)
        final = h == len(pieces) - 1
        if final:
            edges[-1].wait()
            for k in range(CH):
                image_ref[k, R:R + 1, :] = jnp.where(me < F - 1, low_ref[k:k + 1, :], 0.0)
        first = max(start // BLOCK - 1, 0)
        end = (start + size) // BLOCK - (0 if final else 1)
        shrink(first, end)

    for h, (start, size) in enumerate(pieces):
        for copy in back[h]:
            copy.wait()

        @pl.loop(0, size // 8)
        def _(t):
            rows = pl.ds(pl.multiple_of(start + t * 8, 8), 8)
            target = pl.ds(pl.multiple_of(t * 8, 8), 8)
            for c in range(C):
                re_at, im_at = pl.ds(c * W, LANES), pl.ds(c * W + LANES, LANES)
                values = [(recvy[j, rows, re_at], recvy[j, rows, im_at]) for j in range(F)]
                for b, (re, im) in enumerate(block_dft(values, 1.0)):
                    z[b, target, re_at] = re
                    z[b, target, im_at] = im

        span = pl.ds(start, size)

        @pl.loop(0, F, unroll=F)
        def _(b):
            line = exact_dot((t_ref[0, b], t_ref[1, b]), halves(z[b]), ((1,), (1,)))
            gt[pl.ds(b, A, stride=F), :] = line * scale

        for e in range(CH):
            edge[h, e] = gt[e * T:e * T + 8, :]
        for j in range(N // LANES):
            g[span, j * LANES:(j + 1) * LANES] = gt[j * LANES:(j + 1) * LANES, :].T[0:size, :]
        for o in range(1, CH):
            d = lax.rem(mine + o, CH)
            last[h].append(pltpu.make_async_remote_copy(
                src_ref=g.at[span, pl.ds(pl.multiple_of(d * T, LANES), T)],
                dst_ref=grad_ref.at[mine, span],
                send_sem=cs.at[h, o], recv_sem=cr.at[h, o],
                device_id={"chan": d}, device_id_type=pl.DeviceIdType.MESH,
            ))
            last[h].append(halo_copy(
                edge.at[h, lax.rem(mine + o + 1, CH)], edge_ref.at[mine, h],
                rs.at[h, o], rr.at[h, o], {"chan": d},
            ))
        last[h].append(pltpu.make_async_copy(
            g.at[span, pl.ds(pl.multiple_of(mine * T, LANES), T)],
            grad_ref.at[mine, span], ls.at[1 + h],
        ))
        last[h].append(pltpu.make_async_copy(
            edge.at[h, after], edge_ref.at[mine, h], rr.at[h, 0]
        ))
        for copy in last[h]:
            copy.start()
        if h >= 2:
            finish(h - 2)
    for h in range(max(len(pieces) - 2, 0), len(pieces)):
        finish(h)


def place(image, dual, image_out, dual_out, sem):
    copies = [
        pltpu.make_async_copy(image, image_out, sem.at[0]),
        pltpu.make_async_copy(dual, dual_out, sem.at[1]),
    ]
    for copy in copies:
        copy.start()
    for copy in copies:
        copy.wait()


def shards(image, weights, measured, dual):
    F, CH = lax.axis_size("facet"), lax.axis_size("chan")
    R, N = image.shape[1:]
    A = N // F
    C = A // LANES
    RC = R // LANES
    seed, turn, table = (jnp.asarray(t) for t in table_seeds(F, A))
    PC = len(back_pieces(R))
    T = N // CH
    HR = -(-CH // 8) * 8
    f32 = jnp.float32
    dma = pltpu.SemaphoreType.DMA
    vmem = pl.BlockSpec(memory_space=pltpu.VMEM)
    hbm = pl.BlockSpec(memory_space=pl.ANY)
    main = pl.BlockSpec(memory_space=pltpu.HBM)
    staged = pl.pallas_call(
        partial(kernel, F, CH),
        out_shape=(
            pltpu.VMEM((CH, R, T), f32),
            pltpu.VMEM((CH, 2, R, T), jnp.bfloat16),
        ),
        in_specs=[main, vmem, vmem, main, main, main, main],
        out_specs=(vmem, vmem),
        scratch_shapes=[
            pltpu.VMEM((2, F, A, 2 * A), jnp.bfloat16),
            pltpu.VMEM((R, N), f32),
            pltpu.VMEM((CH, R + 8, T), f32),
            pltpu.VMEM((HR, T), f32),
            pltpu.VMEM((HR, T), f32),
            pltpu.VMEM((HR, T), f32),
            pltpu.VMEM((HR, T), f32),
            pltpu.VMEM((CH, R, LANES), f32),
            pltpu.VMEM((CH, R, LANES), f32),
            pltpu.VMEM((CH, R, LANES), f32),
            pltpu.VMEM((CH, R, LANES), f32),
            pltpu.VMEM((PC, CH, 8, LANES), f32),
            pltpu.VMEM((CH, PC, 8, LANES), f32),
            pltpu.VMEM((R, LANES), f32),
            pltpu.VMEM((CH, 2, BLOCK, T), f32),
            pltpu.VMEM((RC, N, LANES), f32),
            pltpu.VMEM((F, LANES, 2 * A), f32),
            pltpu.VMEM((C, F, R, 2 * LANES), f32),
            pltpu.VMEM((C, F, R, 2 * LANES), f32),
            pltpu.VMEM((N, A), jnp.bfloat16),
            pltpu.VMEM((2, N, A), jnp.bfloat16),
            pltpu.VMEM((C, N, LANES), f32),
            pltpu.VMEM((C, 2, N, LANES), f32),
            pltpu.VMEM((F, A, 2 * LANES), f32),
            pltpu.VMEM((F, R, 2 * A), f32),
            pltpu.VMEM((F, R, 2 * A), f32),
            pltpu.VMEM((N, LANES), f32),
            pltpu.VMEM((R, N), f32),
            dma((7 + RC,)),
            dma((C, RC, F)), dma((C, RC, F)),
            dma((C, PC, F)), dma((C, PC, F)),
            dma((PC, CH)), dma((PC, CH)),
            dma((CH,)), dma((CH,)),
            dma((1 + PC,)),
            dma((4,)), dma((4,)),
            dma((PC, CH)), dma((PC, CH)),
        ],
        compiler_params=pltpu.CompilerParams(
            collective_id=0, has_side_effects=True, vmem_limit_bytes=54 * 1024 * 1024
        ),
    )(image[0], seed, turn, table, weights, measured, dual)
    return pl.pallas_call(
        place,
        out_shape=tuple(jax.ShapeDtypeStruct(a.shape, a.dtype) for a in staged),
        in_specs=[hbm, hbm],
        out_specs=(hbm, hbm),
        scratch_shapes=[dma((2,))],
        compiler_params=pltpu.CompilerParams(vmem_limit_bytes=2 * 1024 * 1024),
    )(*staged)


def solution(mesh):
    placed = (
        P("chan", "facet", None),
        P("chan", None, "facet"),
        P("chan", None, None, "facet"),
        P(None, None, "facet", "chan"),
    )
    return jax.shard_map(
        shards,
        mesh=mesh,
        in_specs=placed,
        out_specs=(P(None, "facet", "chan"), P(None, None, "facet", "chan")),
        check_vma=False,
    )
```

```python
from functools import partial
import math

import jax
import jax.numpy as jnp
import numpy as np
from jax import lax
from jax.experimental import pallas as pl
from jax.experimental.pallas import tpu as pltpu
from jax.sharding import PartitionSpec as P

step_primal = 0.5
step_dual = 0.5
clip_radius = 4.0
LANES = 128
BLOCK = 16


def turned(real, imag, num, den, sign):
    num = num % den
    if num == 0:
        return real, imag
    if 4 * num == den:
        return (-imag, real) if sign > 0 else (imag, -real)
    c = math.cos(2.0 * math.pi * num / den)
    s = sign * math.sin(2.0 * math.pi * num / den)
    if 8 * num == den:
        h = math.sqrt(0.5)
        if sign > 0:
            return (real - imag) * h, (real + imag) * h
        return (real + imag) * h, (imag - real) * h
    return real * c - imag * s, real * s + imag * c


def block_dft(values, sign):
    n = len(values)
    if n == 1:
        return values
    even = block_dft(values[0::2], sign)
    odd = block_dft(values[1::2], sign)
    low, high = [], []
    for k in range(n // 2):
        er, ei = even[k]
        tr, ti = turned(*odd[k], k, n, sign)
        low.append((er + tr, ei + ti))
        high.append((er - tr, ei - ti))
    return low + high


def halves(x):
    high = x.astype(jnp.bfloat16)
    return high, (x - high.astype(jnp.float32)).astype(jnp.bfloat16)


def exact_dot(first, second, dims):
    (fh, fl), (sh, sl) = first, second
    dot = partial(
        lax.dot_general, dimension_numbers=(dims, ((), ())), preferred_element_type=jnp.float32
    )
    return dot(fh, sh) + (dot(fh, sl) + dot(fl, sh))


def table_seeds(blocks, inner):
    n = blocks * inner
    a = np.arange(max(blocks, inner))[:, None]
    i = np.arange(inner)[None, :]

    def pairs(step, count):
        phase = 2.0 * np.pi / n * ((step * a[:count] * i) % n)
        pair = np.stack([np.cos(phase), -np.sin(phase)], axis=1).astype(np.float32)
        pair = pair.reshape(count, 2, inner // LANES, LANES)
        return pair.transpose(0, 2, 1, 3).reshape(count, 2 * inner)

    phase = 2.0 * np.pi / n * ((blocks * a[None, :inner] + a[:blocks, None]) * i[:, :LANES] % n)
    value = np.concatenate([np.cos(phase), -np.sin(phase)], axis=2).astype(np.float32)
    high = value.astype(jnp.bfloat16)
    low = (value - high.astype(np.float32)).astype(jnp.bfloat16)
    return pairs(blocks, inner), np.repeat(pairs(1, blocks)[:, None, :], 8, axis=1), np.stack([high, low])


def fill_tables(seed_ref, turn_ref, t_ref):
    _, F, A, width = t_ref.shape

    @pl.loop(0, F)
    def _(b):
        for c in range(1, width // (2 * LANES)):
            re_at = slice(2 * c * LANES, (2 * c + 1) * LANES)
            im_at = slice((2 * c + 1) * LANES, (2 * c + 2) * LANES)
            turn_re, turn_im = turn_ref[b, 0:1, re_at], turn_ref[b, 0:1, im_at]

            @pl.loop(0, A // 32)
            def _(t):
                rows = pl.ds(pl.multiple_of(t * 32, 32), 32)
                re, im = seed_ref[rows, re_at], seed_ref[rows, im_at]
                pair = (re * turn_re - im * turn_im, re * turn_im + im * turn_re)
                for value, at in zip(pair, (re_at, im_at)):
                    high, low = halves(value)
                    t_ref[0, b, rows, at] = high
                    t_ref[1, b, rows, at] = low


def back_pieces(rows):
    pieces, start = [], 0
    while rows - start > 2 * BLOCK:
        size = (rows - start) // 2
        pieces.append((start, size))
        start += size
    return pieces + [(start, rows - start)]


def square_tables(t_ref, k, chunks):
    found = []
    for at in (0, LANES):
        pieces = [
            [t_ref[s, k, :, 2 * LANES * c + at:2 * LANES * c + at + LANES] for c in range(chunks)]
            for s in (0, 1)
        ]
        found.append(tuple(jnp.concatenate(p, axis=1) if chunks > 1 else p[0] for p in pieces))
    return found


def halo_copy(source, target, send_sem, recv_sem, device):
    return pltpu.make_async_remote_copy(
        src_ref=source, dst_ref=target, send_sem=send_sem, recv_sem=recv_sem,
        device_id=device, device_id_type=pl.DeviceIdType.MESH,
    )


def kernel(
    F, CH, x_hbm, seed_ref, turn_ref, table_hbm, w_hbm, m_hbm, d_hbm,
    grad_ref, dual,
    t_ref, x_ref, image_ref, up, up_ref, low, low_ref,
    left, left_ref, right, right_ref, edge, edge_ref, column, parts,
    xt, z, send, recv, wb, mb, wf, mf, u, sendy, recvy, gt, g,
    in_sem, fs, fr, bs, br, cs, cr, xs, xr, ls, hs, hr, rs, rr,
):
    R, N = x_ref.shape
    A = N // F
    C = A // LANES
    T = N // CH
    RC = R // LANES
    W = 2 * LANES
    scale = 1.0 / N
    me = lax.axis_index("facet")
    mine = lax.axis_index("chan")
    order = sorted(range(1, F), key=lambda o: abs(o - F // 2))

    load_x = [
        pltpu.make_async_copy(
            x_hbm.at[h * LANES:(h + 1) * LANES], x_ref.at[h * LANES:(h + 1) * LANES],
            in_sem.at[6 + h],
        )
        for h in range(RC)
    ]
    load_t = pltpu.make_async_copy(table_hbm, t_ref.at[:, :, :, 0:W], in_sem.at[6 + RC])
    load_x[0].start()
    load_t.start()
    for copy in load_x[1:]:
        copy.start()
    load_w = pltpu.make_async_copy(w_hbm.at[0], wb, in_sem.at[0])
    load_m = pltpu.make_async_copy(m_hbm.at[0], mb, in_sem.at[1])
    load_w.start()
    load_m.start()
    load_d = pltpu.make_async_copy(d_hbm, dual, in_sem.at[2])
    load_d.start()
    above, below = lax.rem(me + F - 1, F), lax.rem(me + 1, F)
    before, after = lax.rem(mine + CH - 1, CH), lax.rem(mine + 1, CH)

    barrier = pltpu.get_barrier_semaphore()
    for o in range(1, F):
        pl.semaphore_signal(
            barrier, inc=1, device_id={"facet": lax.rem(me + o, F)},
            device_id_type=pl.DeviceIdType.MESH,
        )
    for o in range(1, CH):
        pl.semaphore_signal(
            barrier, inc=1, device_id={"chan": lax.rem(mine + o, CH)},
            device_id_type=pl.DeviceIdType.MESH,
        )

    copies = []
    for c in range(C):
        wide = slice(c * W, (c + 1) * W)
        group = []
        for h in range(RC):
            if c == 0:
                load_x[h].wait()
                for j in range(N // LANES):
                    xt[h, j * LANES:(j + 1) * LANES, :] = x_ref[
                        h * LANES:(h + 1) * LANES, j * LANES:(j + 1) * LANES
                    ].T

            if c == 0 and h == 0:
                load_t.wait()

            @pl.loop(0, F)
            def _(b):
                part = halves(xt[h, pl.ds(b, A, stride=F), :].T)
                table = (t_ref[0, b, :, wide], t_ref[1, b, :, wide])
                z[b, 0:LANES, 0:W] = exact_dot(part, table, ((1,), (0,)))

            @pl.loop(0, LANES // 8)
            def _(t):
                rows = pl.ds(pl.multiple_of(t * 8, 8), 8)
                target = pl.ds(pl.multiple_of(h * LANES + t * 8, 8), 8)
                values = [(z[b, rows, 0:LANES], z[b, rows, LANES:W]) for b in range(F)]
                for j, (re, im) in enumerate(block_dft(values, -1.0)):
                    send[c, j, target, 0:LANES] = re
                    send[c, j, target, LANES:W] = im

            if c == 0 and h == 0:
                pl.semaphore_wait(barrier, F - 1 + CH - 1)
            span = pl.ds(h * LANES, LANES)
            for o in order:
                d = lax.rem(me + o, F)
                copy = pltpu.make_async_remote_copy(
                    src_ref=send.at[c, d, span], dst_ref=recv.at[c, me, span],
                    send_sem=fs.at[c, h, o], recv_sem=fr.at[c, h, o],
                    device_id={"facet": d}, device_id_type=pl.DeviceIdType.MESH,
                )
                copy.start()
                group.append(copy)
            copy = pltpu.make_async_copy(
                send.at[c, me, span], recv.at[c, me, span], fr.at[c, h, 0]
            )
            copy.start()
            group.append(copy)
        copies.append(group)
        if c == 0:
            fill_tables(seed_ref, turn_ref, t_ref)
            load_d.wait()
            for k in range(CH):
                up[k:k + 1, :] = dual[k, 0, R - 16:R, :].astype(jnp.float32)[15:16, :]
                left[k] = dual[k, 1, :, T - LANES:T].astype(jnp.float32)
            halos = [
                halo_copy(up, up_ref, hs.at[0], hr.at[0], {"facet": below}),
                halo_copy(left, left_ref, hs.at[1], hr.at[1], {"chan": after}),
            ]
            for copy in halos:
                copy.start()

            image_copies = []
            for o in range(1, CH):
                d = lax.rem(mine + o, CH)
                copy = pltpu.make_async_remote_copy(
                    src_ref=x_ref.at[:, pl.ds(pl.multiple_of(d * T, LANES), T)],
                    dst_ref=image_ref.at[mine, 0:R],
                    send_sem=xs.at[o], recv_sem=xr.at[o],
                    device_id={"chan": d}, device_id_type=pl.DeviceIdType.MESH,
                )
                copy.start()
                image_copies.append(copy)
            own = pltpu.make_async_copy(
                x_ref.at[:, pl.ds(pl.multiple_of(mine * T, LANES), T)], image_ref.at[mine, 0:R], ls.at[0]
            )
            own.start()
            image_copies.append(own)

    load_w.wait()
    load_m.wait()

    @pl.loop(0, N // 16)
    def _(t):
        rows = pl.ds(pl.multiple_of(t * 16, 16), 16)
        for c in range(C):
            lo = c * LANES
            wf[c, rows, :] = wb[rows, lo:lo + LANES].astype(jnp.float32) * scale
            mf[c, 0, rows, :] = mb[0, rows, lo:lo + LANES].astype(jnp.float32)
            mf[c, 1, rows, :] = mb[1, rows, lo:lo + LANES].astype(jnp.float32)

    pieces = back_pieces(R)
    back = [[] for _ in pieces]
    for c in range(C):
        wide = slice(c * W, (c + 1) * W)
        for copy in copies[c]:
            copy.wait()

        @pl.loop(0, R // 8)
        def _(t):
            rows = pl.ds(pl.multiple_of(t * 8, 8), 8)
            values = [(recv[c, q, rows, 0:LANES], recv[c, q, rows, LANES:W]) for q in range(F)]
            for k, (re, im) in enumerate(block_dft(values, -1.0)):
                u[k, rows, 0:LANES] = re
                u[k, rows, LANES:W] = im

        @pl.loop(0, F)
        def _(k):
            cos, sin = square_tables(t_ref, k, C)
            part = halves(u[k])
            p = exact_dot(cos, part, ((1,), (0,)))
            q = exact_dot(sin, part, ((1,), (0,)))
            spec_re = p[:, 0:LANES] - q[:, LANES:]
            spec_im = p[:, LANES:] + q[:, 0:LANES]
            lines = pl.ds(k, A, stride=F)
            weight = wf[c, lines, :]
            res_re = weight * spec_re - mf[c, 0, lines, :]
            res_im = weight * spec_im - mf[c, 1, lines, :]
            part = halves(jnp.concatenate([res_re, res_im], axis=1))
            p = exact_dot(cos, part, ((0,), (0,)))
            q = exact_dot(sin, part, ((0,), (0,)))
            u[k, :, 0:LANES] = p[:, 0:LANES] + q[:, LANES:]
            u[k, :, LANES:W] = p[:, LANES:] - q[:, 0:LANES]

        @pl.loop(0, R // 8)
        def _(t):
            rows = pl.ds(pl.multiple_of(t * 8, 8), 8)
            values = [(u[k, rows, 0:LANES], u[k, rows, LANES:W]) for k in range(F)]
            for q, (re, im) in enumerate(block_dft(values, 1.0)):
                sendy[q, rows, c * W:c * W + LANES] = re
                sendy[q, rows, c * W + LANES:(c + 1) * W] = im

        parcels = [(0, pieces[0], wide)]
        if c == C - 1:
            parcels += [(i, piece, slice(0, C * W)) for i, piece in enumerate(pieces) if i > 0]
        for i, (start, size), across in parcels:
            span = pl.ds(start, size)
            for o in order:
                d = lax.rem(me + o, F)
                copy = pltpu.make_async_remote_copy(
                    src_ref=sendy.at[d, span, across], dst_ref=recvy.at[me, span, across],
                    send_sem=bs.at[c, i, o], recv_sem=br.at[c, i, o],
                    device_id={"facet": d}, device_id_type=pl.DeviceIdType.MESH,
                )
                copy.start()
                back[i].append(copy)
            copy = pltpu.make_async_copy(
                sendy.at[me, span, across], recvy.at[me, span, across], br.at[c, i, 0]
            )
            copy.start()
            back[i].append(copy)

        if c == 0:
            for copy in image_copies + halos:
                copy.wait()
            for k in range(CH):
                first_up = jnp.where(me > 0, up_ref[k:k + 1, 0:LANES], 0.0)
                first_left = jnp.where(mine > 0, left_ref[k], 0.0)[:, LANES - 1:LANES]
                p = dual[k, 0, :, 0:LANES].astype(jnp.float32)
                q = dual[k, 1, :, 0:LANES].astype(jnp.float32)
                row = lax.broadcasted_iota(jnp.int32, (R, LANES), 0)
                p_prev = jnp.where(row == 0, first_up, pltpu.roll(p, 1, 0))
                right[k] = image_ref[k, 0:R, 0:LANES] - (p_prev - p + first_left - q)
            edges = [halo_copy(right, right_ref, hs.at[3], hr.at[3], {"chan": before})]
            for copy in edges:
                copy.start()

    row = lax.broadcasted_iota(jnp.int32, (BLOCK, T), 0)
    lane = lax.broadcasted_iota(jnp.int32, (BLOCK, T), 1)

    def primal(first, end):
        @pl.loop(first, end, unroll=(end - first) if end - first < 4 else 1)
        def _(at):
            rows = pl.ds(pl.multiple_of(at * BLOCK, BLOCK), BLOCK)
            ahead = pl.ds(pl.multiple_of(jnp.maximum(at - 1, 0) * BLOCK, BLOCK), BLOCK)
            for k in range(CH):
                p = dual[k, 0, rows, :].astype(jnp.float32)
                q = dual[k, 1, rows, :].astype(jnp.float32)
                top = dual[k, 0, ahead, :].astype(jnp.float32)[BLOCK - 1:BLOCK, :]
                top = jnp.where(at > 0, top, jnp.where(me > 0, up_ref[k:k + 1, :], 0.0))
                p_prev = jnp.where(row == 0, top, pltpu.roll(p, 1, 0))
                start = jnp.where(mine > 0, left_ref[k, rows, :], 0.0)[:, LANES - 1:LANES]
                q_prev = jnp.where(lane == 0, start, pltpu.roll(q, 1, 1))
                adjoint = p_prev - p + q_prev - q
                x = image_ref[k, rows, :]
                value = x - step_primal * (grad_ref[k, rows, :] + adjoint)
                grad_ref[k, rows, :] = value
                image_ref[k, rows, :] = 2.0 * value - x

    def shrink(first, end):
        @pl.loop(first, end, unroll=(end - first) if end - first < 4 else 1)
        def _(at):
            rows = pl.ds(pl.multiple_of(at * BLOCK, BLOCK), BLOCK)
            later = pl.ds(pl.multiple_of(at * BLOCK + BLOCK, BLOCK), 8)
            total = jnp.zeros((BLOCK, T), jnp.float32)
            for k in range(CH):
                e = image_ref[k, rows, :]
                following = image_ref[k, later, :][0:1, :]
                down = jnp.where(row == BLOCK - 1, following, pltpu.roll(e, BLOCK - 1, 0)) - e
                side = right_ref[k, rows, :][:, 0:1] - column[rows, :][:, k:k + 1]
                side = jnp.where(mine < CH - 1, side, 0.0)
                over = jnp.where(lane == T - 1, side, pltpu.roll(e, T - 1, 1)) - e
                first_part = dual[k, 0, rows, :].astype(jnp.float32) + step_dual * down
                second_part = dual[k, 1, rows, :].astype(jnp.float32) + step_dual * over
                parts[k, 0] = first_part
                parts[k, 1] = second_part
                total = total + (first_part * first_part + second_part * second_part)
            factor = 1.0 / jnp.maximum(1.0, jnp.sqrt(total) / clip_radius)
            for k in range(CH):
                dual[k, 0, rows, :] = (parts[k, 0] * factor).astype(jnp.bfloat16)
                dual[k, 1, rows, :] = (parts[k, 1] * factor).astype(jnp.bfloat16)

    last = [[] for _ in pieces]

    def finish(h):
        start, size = pieces[h]
        for copy in last[h]:
            copy.wait()
        if h == 0:
            for copy in edges:
                copy.wait()
        tile = jnp.concatenate([edge_ref[k, h, 0:1, :] for k in range(CH)], axis=0)
        tile = jnp.concatenate([tile] * (LANES // CH), axis=0)
        column[start:start + size, :] = tile.T[0:size, :]
        primal(start // BLOCK, (start + size) // BLOCK)
        if h == 0:
            for k in range(CH):
                low[k:k + 1, :] = image_ref[k, 0:8, :][0:1, :]
            copy = halo_copy(low, low_ref, hs.at[2], hr.at[2], {"facet": above})
            copy.start()
            edges.append(copy)
        final = h == len(pieces) - 1
        if final:
            edges[-1].wait()
            for k in range(CH):
                image_ref[k, R:R + 1, :] = jnp.where(me < F - 1, low_ref[k:k + 1, :], 0.0)
        first = max(start // BLOCK - 1, 0)
        end = (start + size) // BLOCK - (0 if final else 1)
        shrink(first, end)

    for h, (start, size) in enumerate(pieces):
        for copy in back[h]:
            copy.wait()

        @pl.loop(0, size // 8)
        def _(t):
            rows = pl.ds(pl.multiple_of(start + t * 8, 8), 8)
            target = pl.ds(pl.multiple_of(t * 8, 8), 8)
            for c in range(C):
                re_at, im_at = pl.ds(c * W, LANES), pl.ds(c * W + LANES, LANES)
                values = [(recvy[j, rows, re_at], recvy[j, rows, im_at]) for j in range(F)]
                for b, (re, im) in enumerate(block_dft(values, 1.0)):
                    z[b, target, re_at] = re
                    z[b, target, im_at] = im

        span = pl.ds(start, size)

        @pl.loop(0, F, unroll=F)
        def _(b):
            line = exact_dot((t_ref[0, b], t_ref[1, b]), halves(z[b]), ((1,), (1,)))
            gt[pl.ds(b, A, stride=F), :] = line * scale

        for e in range(CH):
            edge[h, e] = gt[e * T:e * T + 8, :]
        for j in range(N // LANES):
            g[span, j * LANES:(j + 1) * LANES] = gt[j * LANES:(j + 1) * LANES, :].T[0:size, :]
        for o in range(1, CH):
            d = lax.rem(mine + o, CH)
            last[h].append(pltpu.make_async_remote_copy(
                src_ref=g.at[span, pl.ds(pl.multiple_of(d * T, LANES), T)],
                dst_ref=grad_ref.at[mine, span],
                send_sem=cs.at[h, o], recv_sem=cr.at[h, o],
                device_id={"chan": d}, device_id_type=pl.DeviceIdType.MESH,
            ))
            last[h].append(halo_copy(
                edge.at[h, lax.rem(mine + o + 1, CH)], edge_ref.at[mine, h],
                rs.at[h, o], rr.at[h, o], {"chan": d},
            ))
        last[h].append(pltpu.make_async_copy(
            g.at[span, pl.ds(pl.multiple_of(mine * T, LANES), T)],
            grad_ref.at[mine, span], ls.at[1 + h],
        ))
        last[h].append(pltpu.make_async_copy(
            edge.at[h, after], edge_ref.at[mine, h], rr.at[h, 0]
        ))
        for copy in last[h]:
            copy.start()
        if h >= 2:
            finish(h - 2)
    for h in range(max(len(pieces) - 2, 0), len(pieces)):
        finish(h)


def place(image, dual, image_out, dual_out, sem):
    copies = []
    for k in range(image.shape[0]):
        copies += [
            pltpu.make_async_copy(image.at[k], image_out.at[k], sem.at[0, k]),
            pltpu.make_async_copy(dual.at[k], dual_out.at[k], sem.at[1, k]),
        ]
    for copy in copies:
        copy.start()
    for copy in copies:
        copy.wait()


def shards(image, weights, measured, dual):
    F, CH = lax.axis_size("facet"), lax.axis_size("chan")
    R, N = image.shape[1:]
    A = N // F
    C = A // LANES
    RC = R // LANES
    seed, turn, table = (jnp.asarray(t) for t in table_seeds(F, A))
    PC = len(back_pieces(R))
    T = N // CH
    HR = -(-CH // 8) * 8
    f32 = jnp.float32
    dma = pltpu.SemaphoreType.DMA
    vmem = pl.BlockSpec(memory_space=pltpu.VMEM)
    hbm = pl.BlockSpec(memory_space=pl.ANY)
    main = pl.BlockSpec(memory_space=pltpu.HBM)
    staged = pl.pallas_call(
        partial(kernel, F, CH),
        out_shape=(
            pltpu.VMEM((CH, R, T), f32),
            pltpu.VMEM((CH, 2, R, T), jnp.bfloat16),
        ),
        in_specs=[main, vmem, vmem, main, main, main, main],
        out_specs=(vmem, vmem),
        scratch_shapes=[
            pltpu.VMEM((2, F, A, 2 * A), jnp.bfloat16),
            pltpu.VMEM((R, N), f32),
            pltpu.VMEM((CH, R + 8, T), f32),
            pltpu.VMEM((HR, T), f32),
            pltpu.VMEM((HR, T), f32),
            pltpu.VMEM((HR, T), f32),
            pltpu.VMEM((HR, T), f32),
            pltpu.VMEM((CH, R, LANES), f32),
            pltpu.VMEM((CH, R, LANES), f32),
            pltpu.VMEM((CH, R, LANES), f32),
            pltpu.VMEM((CH, R, LANES), f32),
            pltpu.VMEM((PC, CH, 8, LANES), f32),
            pltpu.VMEM((CH, PC, 8, LANES), f32),
            pltpu.VMEM((R, LANES), f32),
            pltpu.VMEM((CH, 2, BLOCK, T), f32),
            pltpu.VMEM((RC, N, LANES), f32),
            pltpu.VMEM((F, LANES, 2 * A), f32),
            pltpu.VMEM((C, F, R, 2 * LANES), f32),
            pltpu.VMEM((C, F, R, 2 * LANES), f32),
            pltpu.VMEM((N, A), jnp.bfloat16),
            pltpu.VMEM((2, N, A), jnp.bfloat16),
            pltpu.VMEM((C, N, LANES), f32),
            pltpu.VMEM((C, 2, N, LANES), f32),
            pltpu.VMEM((F, A, 2 * LANES), f32),
            pltpu.VMEM((F, R, 2 * A), f32),
            pltpu.VMEM((F, R, 2 * A), f32),
            pltpu.VMEM((N, LANES), f32),
            pltpu.VMEM((R, N), f32),
            dma((7 + RC,)),
            dma((C, RC, F)), dma((C, RC, F)),
            dma((C, PC, F)), dma((C, PC, F)),
            dma((PC, CH)), dma((PC, CH)),
            dma((CH,)), dma((CH,)),
            dma((1 + PC,)),
            dma((4,)), dma((4,)),
            dma((PC, CH)), dma((PC, CH)),
        ],
        compiler_params=pltpu.CompilerParams(
            collective_id=0, has_side_effects=True, vmem_limit_bytes=54 * 1024 * 1024
        ),
    )(image[0], seed, turn, table, weights, measured, dual)
    return pl.pallas_call(
        place,
        out_shape=tuple(jax.ShapeDtypeStruct(a.shape, a.dtype) for a in staged),
        in_specs=[hbm, hbm],
        out_specs=(hbm, hbm),
        scratch_shapes=[dma((2, CH))],
        compiler_params=pltpu.CompilerParams(vmem_limit_bytes=2 * 1024 * 1024),
    )(*staged)


def solution(mesh):
    placed = (
        P("chan", "facet", None),
        P("chan", None, "facet"),
        P("chan", None, None, "facet"),
        P(None, None, "facet", "chan"),
    )
    return jax.shard_map(
        shards,
        mesh=mesh,
        in_specs=placed,
        out_specs=(P(None, "facet", "chan"), P(None, None, "facet", "chan")),
        check_vma=False,
    )
```

```python
from functools import partial
import math

import jax
import jax.numpy as jnp
import numpy as np
from jax import lax
from jax.experimental import pallas as pl
from jax.experimental.pallas import tpu as pltpu
from jax.sharding import PartitionSpec as P

step_primal = 0.5
step_dual = 0.5
clip_radius = 4.0
LANES = 128
BLOCK = 16


def turned(real, imag, num, den, sign):
    num = num % den
    if num == 0:
        return real, imag
    if 4 * num == den:
        return (-imag, real) if sign > 0 else (imag, -real)
    c = math.cos(2.0 * math.pi * num / den)
    s = sign * math.sin(2.0 * math.pi * num / den)
    if 8 * num == den:
        h = math.sqrt(0.5)
        if sign > 0:
            return (real - imag) * h, (real + imag) * h
        return (real + imag) * h, (imag - real) * h
    return real * c - imag * s, real * s + imag * c


def block_dft(values, sign):
    n = len(values)
    if n == 1:
        return values
    even = block_dft(values[0::2], sign)
    odd = block_dft(values[1::2], sign)
    low, high = [], []
    for k in range(n // 2):
        er, ei = even[k]
        tr, ti = turned(*odd[k], k, n, sign)
        low.append((er + tr, ei + ti))
        high.append((er - tr, ei - ti))
    return low + high


def halves(x):
    high = x.astype(jnp.bfloat16)
    return high, (x - high.astype(jnp.float32)).astype(jnp.bfloat16)


def exact_dot(first, second, dims):
    (fh, fl), (sh, sl) = first, second
    dot = partial(
        lax.dot_general, dimension_numbers=(dims, ((), ())), preferred_element_type=jnp.float32
    )
    return dot(fh, sh) + (dot(fh, sl) + dot(fl, sh))


def table_seeds(blocks, inner):
    n = blocks * inner
    a = np.arange(max(blocks, inner))[:, None]
    i = np.arange(inner)[None, :]

    def pairs(step, count):
        phase = 2.0 * np.pi / n * ((step * a[:count] * i) % n)
        pair = np.stack([np.cos(phase), -np.sin(phase)], axis=1).astype(np.float32)
        pair = pair.reshape(count, 2, inner // LANES, LANES)
        return pair.transpose(0, 2, 1, 3).reshape(count, 2 * inner)

    phase = 2.0 * np.pi / n * ((blocks * a[None, :inner] + a[:blocks, None]) * i[:, :LANES] % n)
    value = np.concatenate([np.cos(phase), -np.sin(phase)], axis=2).astype(np.float32)
    high = value.astype(jnp.bfloat16)
    low = (value - high.astype(np.float32)).astype(jnp.bfloat16)
    return pairs(blocks, inner), np.repeat(pairs(1, blocks)[:, None, :], 8, axis=1), np.stack([high, low])


def fill_tables(seed_ref, turn_ref, t_ref):
    _, F, A, width = t_ref.shape

    @pl.loop(0, F)
    def _(b):
        for c in range(1, width // (2 * LANES)):
            re_at = slice(2 * c * LANES, (2 * c + 1) * LANES)
            im_at = slice((2 * c + 1) * LANES, (2 * c + 2) * LANES)
            turn_re, turn_im = turn_ref[b, 0:1, re_at], turn_ref[b, 0:1, im_at]

            @pl.loop(0, A // 32)
            def _(t):
                rows = pl.ds(pl.multiple_of(t * 32, 32), 32)
                re, im = seed_ref[rows, re_at], seed_ref[rows, im_at]
                pair = (re * turn_re - im * turn_im, re * turn_im + im * turn_re)
                for value, at in zip(pair, (re_at, im_at)):
                    high, low = halves(value)
                    t_ref[0, b, rows, at] = high
                    t_ref[1, b, rows, at] = low


def back_pieces(rows):
    pieces, start = [], 0
    while rows - start > 2 * BLOCK:
        size = (rows - start) // 2
        pieces.append((start, size))
        start += size
    return pieces + [(start, rows - start)]


def square_tables(t_ref, k, chunks):
    found = []
    for at in (0, LANES):
        pieces = [
            [t_ref[s, k, :, 2 * LANES * c + at:2 * LANES * c + at + LANES] for c in range(chunks)]
            for s in (0, 1)
        ]
        found.append(tuple(jnp.concatenate(p, axis=1) if chunks > 1 else p[0] for p in pieces))
    return found


def halo_copy(source, target, send_sem, recv_sem, device):
    return pltpu.make_async_remote_copy(
        src_ref=source, dst_ref=target, send_sem=send_sem, recv_sem=recv_sem,
        device_id=device, device_id_type=pl.DeviceIdType.MESH,
    )


def kernel(
    F, CH, x_hbm, seed_ref, turn_ref, table_hbm, w_hbm, m_hbm, d_hbm,
    grad_ref, dual,
    t_ref, x_ref, image_ref, up, up_ref, low, low_ref,
    left, left_ref, right, right_ref, edge, edge_ref, column, parts,
    xt, z, send, recv, wb, mb, wf, mf, u, sendy, recvy, gt, g,
    in_sem, fs, fr, bs, br, cs, cr, xs, xr, ls, hs, hr, rs, rr,
):
    R, N = x_ref.shape
    A = N // F
    C = A // LANES
    T = N // CH
    RC = R // LANES
    W = 2 * LANES
    scale = 1.0 / N
    me = lax.axis_index("facet")
    mine = lax.axis_index("chan")
    order = sorted(range(1, F), key=lambda o: abs(o - F // 2))

    load_x = [
        pltpu.make_async_copy(
            x_hbm.at[h * LANES:(h + 1) * LANES], x_ref.at[h * LANES:(h + 1) * LANES],
            in_sem.at[6 + h],
        )
        for h in range(RC)
    ]
    load_t = pltpu.make_async_copy(table_hbm, t_ref.at[:, :, :, 0:W], in_sem.at[6 + RC])
    load_x[0].start()
    load_t.start()
    for copy in load_x[1:]:
        copy.start()
    load_w = pltpu.make_async_copy(w_hbm.at[0], wb, in_sem.at[0])
    load_m = pltpu.make_async_copy(m_hbm.at[0], mb, in_sem.at[1])
    load_w.start()
    load_m.start()
    load_d = pltpu.make_async_copy(d_hbm, dual, in_sem.at[2])
    load_d.start()
    above, below = lax.rem(me + F - 1, F), lax.rem(me + 1, F)
    before, after = lax.rem(mine + CH - 1, CH), lax.rem(mine + 1, CH)

    barrier = pltpu.get_barrier_semaphore()
    for o in range(1, F):
        pl.semaphore_signal(
            barrier, inc=1, device_id={"facet": lax.rem(me + o, F)},
            device_id_type=pl.DeviceIdType.MESH,
        )
    for o in range(1, CH):
        pl.semaphore_signal(
            barrier, inc=1, device_id={"chan": lax.rem(mine + o, CH)},
            device_id_type=pl.DeviceIdType.MESH,
        )

    copies = []
    for c in range(C):
        wide = slice(c * W, (c + 1) * W)
        group = []
        for h in range(RC):
            if c == 0:
                load_x[h].wait()
                for j in range(N // LANES):
                    xt[h, j * LANES:(j + 1) * LANES, :] = x_ref[
                        h * LANES:(h + 1) * LANES, j * LANES:(j + 1) * LANES
                    ].T

            if c == 0 and h == 0:
                load_t.wait()

            @pl.loop(0, F)
            def _(b):
                part = halves(xt[h, pl.ds(b, A, stride=F), :].T)
                table = (t_ref[0, b, :, wide], t_ref[1, b, :, wide])
                z[b, 0:LANES, 0:W] = exact_dot(part, table, ((1,), (0,)))

            @pl.loop(0, LANES // 8)
            def _(t):
                rows = pl.ds(pl.multiple_of(t * 8, 8), 8)
                target = pl.ds(pl.multiple_of(h * LANES + t * 8, 8), 8)
                values = [(z[b, rows, 0:LANES], z[b, rows, LANES:W]) for b in range(F)]
                for j, (re, im) in enumerate(block_dft(values, -1.0)):
                    send[c, j, target, 0:LANES] = re
                    send[c, j, target, LANES:W] = im

            if c == 0 and h == 0:
                pl.semaphore_wait(barrier, F - 1 + CH - 1)
            span = pl.ds(h * LANES, LANES)
            for o in order:
                d = lax.rem(me + o, F)
                copy = pltpu.make_async_remote_copy(
                    src_ref=send.at[c, d, span], dst_ref=recv.at[c, me, span],
                    send_sem=fs.at[c, h, o], recv_sem=fr.at[c, h, o],
                    device_id={"facet": d}, device_id_type=pl.DeviceIdType.MESH,
                )
                copy.start()
                group.append(copy)
            copy = pltpu.make_async_copy(
                send.at[c, me, span], recv.at[c, me, span], fr.at[c, h, 0]
            )
            copy.start()
            group.append(copy)
        copies.append(group)
        if c == 0:
            fill_tables(seed_ref, turn_ref, t_ref)
            load_d.wait()
            for k in range(CH):
                up[k:k + 1, :] = dual[k, 0, R - 16:R, :].astype(jnp.float32)[15:16, :]
                left[k] = dual[k, 1, :, T - LANES:T].astype(jnp.float32)
            halos = [
                halo_copy(up, up_ref, hs.at[0], hr.at[0], {"facet": below}),
                halo_copy(left, left_ref, hs.at[1], hr.at[1], {"chan": after}),
            ]
            for copy in halos:
                copy.start()

            image_copies = []
            for o in range(1, CH):
                d = lax.rem(mine + o, CH)
                copy = pltpu.make_async_remote_copy(
                    src_ref=x_ref.at[:, pl.ds(pl.multiple_of(d * T, LANES), T)],
                    dst_ref=image_ref.at[mine, 0:R],
                    send_sem=xs.at[o], recv_sem=xr.at[o],
                    device_id={"chan": d}, device_id_type=pl.DeviceIdType.MESH,
                )
                copy.start()
                image_copies.append(copy)
            own = pltpu.make_async_copy(
                x_ref.at[:, pl.ds(pl.multiple_of(mine * T, LANES), T)], image_ref.at[mine, 0:R], ls.at[0]
            )
            own.start()
            image_copies.append(own)

    load_w.wait()
    load_m.wait()

    @pl.loop(0, N // 16)
    def _(t):
        rows = pl.ds(pl.multiple_of(t * 16, 16), 16)
        for c in range(C):
            lo = c * LANES
            wf[c, rows, :] = wb[rows, lo:lo + LANES].astype(jnp.float32) * scale
            mf[c, 0, rows, :] = mb[0, rows, lo:lo + LANES].astype(jnp.float32)
            mf[c, 1, rows, :] = mb[1, rows, lo:lo + LANES].astype(jnp.float32)

    pieces = back_pieces(R)
    back = [[] for _ in pieces]
    for c in range(C):
        wide = slice(c * W, (c + 1) * W)
        for copy in copies[c]:
            copy.wait()

        @pl.loop(0, R // 8)
        def _(t):
            rows = pl.ds(pl.multiple_of(t * 8, 8), 8)
            values = [(recv[c, q, rows, 0:LANES], recv[c, q, rows, LANES:W]) for q in range(F)]
            for k, (re, im) in enumerate(block_dft(values, -1.0)):
                u[k, rows, 0:LANES] = re
                u[k, rows, LANES:W] = im

        @pl.loop(0, F)
        def _(k):
            cos, sin = square_tables(t_ref, k, C)
            part = halves(u[k])
            p = exact_dot(cos, part, ((1,), (0,)))
            q = exact_dot(sin, part, ((1,), (0,)))
            spec_re = p[:, 0:LANES] - q[:, LANES:]
            spec_im = p[:, LANES:] + q[:, 0:LANES]
            lines = pl.ds(k, A, stride=F)
            weight = wf[c, lines, :]
            res_re = weight * spec_re - mf[c, 0, lines, :]
            res_im = weight * spec_im - mf[c, 1, lines, :]
            part = halves(jnp.concatenate([res_re, res_im], axis=1))
            p = exact_dot(cos, part, ((0,), (0,)))
            q = exact_dot(sin, part, ((0,), (0,)))
            u[k, :, 0:LANES] = p[:, 0:LANES] + q[:, LANES:]
            u[k, :, LANES:W] = p[:, LANES:] - q[:, 0:LANES]

        @pl.loop(0, R // 8)
        def _(t):
            rows = pl.ds(pl.multiple_of(t * 8, 8), 8)
            values = [(u[k, rows, 0:LANES], u[k, rows, LANES:W]) for k in range(F)]
            for q, (re, im) in enumerate(block_dft(values, 1.0)):
                sendy[q, rows, c * W:c * W + LANES] = re
                sendy[q, rows, c * W + LANES:(c + 1) * W] = im

        parcels = [(0, pieces[0], wide)]
        if c == C - 1:
            parcels += [(i, piece, slice(0, C * W)) for i, piece in enumerate(pieces) if i > 0]
        for i, (start, size), across in parcels:
            span = pl.ds(start, size)
            for o in order:
                d = lax.rem(me + o, F)
                copy = pltpu.make_async_remote_copy(
                    src_ref=sendy.at[d, span, across], dst_ref=recvy.at[me, span, across],
                    send_sem=bs.at[c, i, o], recv_sem=br.at[c, i, o],
                    device_id={"facet": d}, device_id_type=pl.DeviceIdType.MESH,
                )
                copy.start()
                back[i].append(copy)
            copy = pltpu.make_async_copy(
                sendy.at[me, span, across], recvy.at[me, span, across], br.at[c, i, 0]
            )
            copy.start()
            back[i].append(copy)

        if c == 0:
            for copy in image_copies + halos:
                copy.wait()
            for k in range(CH):
                first_up = jnp.where(me > 0, up_ref[k:k + 1, 0:LANES], 0.0)
                first_left = jnp.where(mine > 0, left_ref[k], 0.0)[:, LANES - 1:LANES]
                p = dual[k, 0, :, 0:LANES].astype(jnp.float32)
                q = dual[k, 1, :, 0:LANES].astype(jnp.float32)
                row = lax.broadcasted_iota(jnp.int32, (R, LANES), 0)
                p_prev = jnp.where(row == 0, first_up, pltpu.roll(p, 1, 0))
                right[k] = image_ref[k, 0:R, 0:LANES] - (p_prev - p + first_left - q)
            edges = [halo_copy(right, right_ref, hs.at[3], hr.at[3], {"chan": before})]
            for copy in edges:
                copy.start()

    row = lax.broadcasted_iota(jnp.int32, (BLOCK, T), 0)
    lane = lax.broadcasted_iota(jnp.int32, (BLOCK, T), 1)

    def primal(first, end):
        @pl.loop(first, end, unroll=(end - first) if end - first < 4 else 1)
        def _(at):
            rows = pl.ds(pl.multiple_of(at * BLOCK, BLOCK), BLOCK)
            ahead = pl.ds(pl.multiple_of(jnp.maximum(at - 1, 0) * BLOCK, BLOCK), BLOCK)
            for k in range(CH):
                p = dual[k, 0, rows, :].astype(jnp.float32)
                q = dual[k, 1, rows, :].astype(jnp.float32)
                top = dual[k, 0, ahead, :].astype(jnp.float32)[BLOCK - 1:BLOCK, :]
                top = jnp.where(at > 0, top, jnp.where(me > 0, up_ref[k:k + 1, :], 0.0))
                p_prev = jnp.where(row == 0, top, pltpu.roll(p, 1, 0))
                start = jnp.where(mine > 0, left_ref[k, rows, :], 0.0)[:, LANES - 1:LANES]
                q_prev = jnp.where(lane == 0, start, pltpu.roll(q, 1, 1))
                adjoint = p_prev - p + q_prev - q
                x = image_ref[k, rows, :]
                value = x - step_primal * (grad_ref[k, rows, :] + adjoint)
                grad_ref[k, rows, :] = value
                image_ref[k, rows, :] = 2.0 * value - x

    def shrink(first, end):
        @pl.loop(first, end, unroll=(end - first) if end - first < 4 else 1)
        def _(at):
            rows = pl.ds(pl.multiple_of(at * BLOCK, BLOCK), BLOCK)
            later = pl.ds(pl.multiple_of(at * BLOCK + BLOCK, BLOCK), 8)
            total = jnp.zeros((BLOCK, T), jnp.float32)
            for k in range(CH):
                e = image_ref[k, rows, :]
                following = image_ref[k, later, :][0:1, :]
                down = jnp.where(row == BLOCK - 1, following, pltpu.roll(e, BLOCK - 1, 0)) - e
                side = right_ref[k, rows, :][:, 0:1] - column[rows, :][:, k:k + 1]
                side = jnp.where(mine < CH - 1, side, 0.0)
                over = jnp.where(lane == T - 1, side, pltpu.roll(e, T - 1, 1)) - e
                first_part = dual[k, 0, rows, :].astype(jnp.float32) + step_dual * down
                second_part = dual[k, 1, rows, :].astype(jnp.float32) + step_dual * over
                parts[k, 0] = first_part
                parts[k, 1] = second_part
                total = total + (first_part * first_part + second_part * second_part)
            factor = 1.0 / jnp.maximum(1.0, jnp.sqrt(total) / clip_radius)
            for k in range(CH):
                dual[k, 0, rows, :] = (parts[k, 0] * factor).astype(jnp.bfloat16)
                dual[k, 1, rows, :] = (parts[k, 1] * factor).astype(jnp.bfloat16)

    last = [[] for _ in pieces]

    def finish(h):
        start, size = pieces[h]
        for copy in last[h]:
            copy.wait()
        if h == 0:
            for copy in edges:
                copy.wait()
        tile = jnp.concatenate([edge_ref[k, h, 0:1, :] for k in range(CH)], axis=0)
        tile = jnp.concatenate([tile] * (LANES // CH), axis=0)
        column[start:start + size, :] = tile.T[0:size, :]
        primal(start // BLOCK, (start + size) // BLOCK)
        if h == 0:
            for k in range(CH):
                low[k:k + 1, :] = image_ref[k, 0:8, :][0:1, :]
            copy = halo_copy(low, low_ref, hs.at[2], hr.at[2], {"facet": above})
            copy.start()
            edges.append(copy)
        final = h == len(pieces) - 1
        if final:
            edges[-1].wait()
            for k in range(CH):
                image_ref[k, R:R + 1, :] = jnp.where(me < F - 1, low_ref[k:k + 1, :], 0.0)
        first = max(start // BLOCK - 1, 0)
        end = (start + size) // BLOCK - (0 if final else 1)
        shrink(first, end)

    for h, (start, size) in enumerate(pieces):
        for copy in back[h]:
            copy.wait()

        @pl.loop(0, size // 8)
        def _(t):
            rows = pl.ds(pl.multiple_of(start + t * 8, 8), 8)
            target = pl.ds(pl.multiple_of(t * 8, 8), 8)
            for c in range(C):
                re_at, im_at = pl.ds(c * W, LANES), pl.ds(c * W + LANES, LANES)
                values = [(recvy[j, rows, re_at], recvy[j, rows, im_at]) for j in range(F)]
                for b, (re, im) in enumerate(block_dft(values, 1.0)):
                    z[b, target, re_at] = re
                    z[b, target, im_at] = im

        span = pl.ds(start, size)

        @pl.loop(0, F, unroll=F)
        def _(b):
            line = exact_dot((t_ref[0, b], t_ref[1, b]), halves(z[b]), ((1,), (1,)))
            gt[pl.ds(b, A, stride=F), :] = line * scale

        for e in range(CH):
            edge[h, e] = gt[e * T:e * T + 8, :]
        for j in range(N // LANES):
            g[span, j * LANES:(j + 1) * LANES] = gt[j * LANES:(j + 1) * LANES, :].T[0:size, :]
        for o in range(1, CH):
            d = lax.rem(mine + o, CH)
            last[h].append(pltpu.make_async_remote_copy(
                src_ref=g.at[span, pl.ds(pl.multiple_of(d * T, LANES), T)],
                dst_ref=grad_ref.at[mine, span],
                send_sem=cs.at[h, o], recv_sem=cr.at[h, o],
                device_id={"chan": d}, device_id_type=pl.DeviceIdType.MESH,
            ))
            last[h].append(halo_copy(
                edge.at[h, lax.rem(mine + o + 1, CH)], edge_ref.at[mine, h],
                rs.at[h, o], rr.at[h, o], {"chan": d},
            ))
        last[h].append(pltpu.make_async_copy(
            g.at[span, pl.ds(pl.multiple_of(mine * T, LANES), T)],
            grad_ref.at[mine, span], ls.at[1 + h],
        ))
        last[h].append(pltpu.make_async_copy(
            edge.at[h, after], edge_ref.at[mine, h], rr.at[h, 0]
        ))
        for copy in last[h]:
            copy.start()
        if h >= 3:
            finish(h - 3)
    for h in range(max(len(pieces) - 3, 0), len(pieces)):
        finish(h)


def place(image, dual, image_out, dual_out, sem):
    copies = []
    for k in range(image.shape[0]):
        copies += [
            pltpu.make_async_copy(image.at[k], image_out.at[k], sem.at[0, k]),
            pltpu.make_async_copy(dual.at[k], dual_out.at[k], sem.at[1, k]),
        ]
    for copy in copies:
        copy.start()
    for copy in copies:
        copy.wait()


def shards(image, weights, measured, dual):
    F, CH = lax.axis_size("facet"), lax.axis_size("chan")
    R, N = image.shape[1:]
    A = N // F
    C = A // LANES
    RC = R // LANES
    seed, turn, table = (jnp.asarray(t) for t in table_seeds(F, A))
    PC = len(back_pieces(R))
    T = N // CH
    HR = -(-CH // 8) * 8
    f32 = jnp.float32
    dma = pltpu.SemaphoreType.DMA
    vmem = pl.BlockSpec(memory_space=pltpu.VMEM)
    hbm = pl.BlockSpec(memory_space=pl.ANY)
    main = pl.BlockSpec(memory_space=pltpu.HBM)
    staged = pl.pallas_call(
        partial(kernel, F, CH),
        out_shape=(
            pltpu.VMEM((CH, R, T), f32),
            pltpu.VMEM((CH, 2, R, T), jnp.bfloat16),
        ),
        in_specs=[main, vmem, vmem, main, main, main, main],
        out_specs=(vmem, vmem),
        scratch_shapes=[
            pltpu.VMEM((2, F, A, 2 * A), jnp.bfloat16),
            pltpu.VMEM((R, N), f32),
            pltpu.VMEM((CH, R + 8, T), f32),
            pltpu.VMEM((HR, T), f32),
            pltpu.VMEM((HR, T), f32),
            pltpu.VMEM((HR, T), f32),
            pltpu.VMEM((HR, T), f32),
            pltpu.VMEM((CH, R, LANES), f32),
            pltpu.VMEM((CH, R, LANES), f32),
            pltpu.VMEM((CH, R, LANES), f32),
            pltpu.VMEM((CH, R, LANES), f32),
            pltpu.VMEM((PC, CH, 8, LANES), f32),
            pltpu.VMEM((CH, PC, 8, LANES), f32),
            pltpu.VMEM((R, LANES), f32),
            pltpu.VMEM((CH, 2, BLOCK, T), f32),
            pltpu.VMEM((RC, N, LANES), f32),
            pltpu.VMEM((F, LANES, 2 * A), f32),
            pltpu.VMEM((C, F, R, 2 * LANES), f32),
            pltpu.VMEM((C, F, R, 2 * LANES), f32),
            pltpu.VMEM((N, A), jnp.bfloat16),
            pltpu.VMEM((2, N, A), jnp.bfloat16),
            pltpu.VMEM((C, N, LANES), f32),
            pltpu.VMEM((C, 2, N, LANES), f32),
            pltpu.VMEM((F, A, 2 * LANES), f32),
            pltpu.VMEM((F, R, 2 * A), f32),
            pltpu.VMEM((F, R, 2 * A), f32),
            pltpu.VMEM((N, LANES), f32),
            pltpu.VMEM((R, N), f32),
            dma((7 + RC,)),
            dma((C, RC, F)), dma((C, RC, F)),
            dma((C, PC, F)), dma((C, PC, F)),
            dma((PC, CH)), dma((PC, CH)),
            dma((CH,)), dma((CH,)),
            dma((1 + PC,)),
            dma((4,)), dma((4,)),
            dma((PC, CH)), dma((PC, CH)),
        ],
        compiler_params=pltpu.CompilerParams(
            collective_id=0, has_side_effects=True, vmem_limit_bytes=54 * 1024 * 1024
        ),
    )(image[0], seed, turn, table, weights, measured, dual)
    return pl.pallas_call(
        place,
        out_shape=tuple(jax.ShapeDtypeStruct(a.shape, a.dtype) for a in staged),
        in_specs=[hbm, hbm],
        out_specs=(hbm, hbm),
        scratch_shapes=[dma((2, CH))],
        compiler_params=pltpu.CompilerParams(vmem_limit_bytes=2 * 1024 * 1024),
    )(*staged)


def solution(mesh):
    placed = (
        P("chan", "facet", None),
        P("chan", None, "facet"),
        P("chan", None, None, "facet"),
        P(None, None, "facet", "chan"),
    )
    return jax.shard_map(
        shards,
        mesh=mesh,
        in_specs=placed,
        out_specs=(P(None, "facet", "chan"), P(None, None, "facet", "chan")),
        check_vma=False,
    )
```
